32 devices in a mesh: dp: 8 (over z, core), expert: 4 (over y, x).
Axes of the slice: x: 2, y: 2, z: 4, core: 2. Of those that a mesh axis runs over, the one named last changes fastest.
Arguments:
- embedded: bfloat16 [64, 197, 512], P(('dp', 'expert')), may hold values from -6 to 6
- cotangent: bfloat16 [64, 197, 512], P(('dp', 'expert')), may hold values from -6 to 6
- w_qkv: bfloat16 [2, 512, 1536], P(None, 'dp'), may hold values from -0.25 to 0.25
- w_proj: bfloat16 [2, 512, 512], P(None, 'dp'), may hold values from -2.5 to 2.5
- w_router: bfloat16 [2, 512, 8], P(None, 'dp'), may hold values from -0.1875 to 0.1875
- norm_gains: bfloat16 [2, 2, 512], P(None, None, 'dp'), may hold values from 0.25 to 1.75
- norm_shifts: bfloat16 [2, 2, 512], P(None, None, 'dp'), may hold values from -1 to 1
- w_first: bfloat16 [2, 8, 512, 2048], P(None, 'expert', None, 'dp'), may hold values from -0.25 to 0.25
- w_second: bfloat16 [2, 8, 2048, 512], P(None, 'expert', 'dp'), may hold values from -1 to 1
- routes: int32 [2, 64, 197, 2], P(None, ('dp', 'expert')), may hold values from 0 to 7, all different within a row; in each aligned block of 394 rows (0 to 393, 394 to 787, ..., all dimensions but the last counted through in order) at most 147 rows name the same one
Outputs:
- out_images: bfloat16 [64, 197, 512], P(('dp', 'expert'))
- grad_images: float32 [64, 197, 512], P(('dp', 'expert'))
- grad_qkv: float32 [2, 512, 1536], P(None, 'dp')
- grad_proj: float32 [2, 512, 512], P(None, 'dp')
- grad_router: float32 [2, 512, 8], P(None, 'dp')
- grad_gains: float32 [2, 2, 512], P(None, None, 'dp')
- grad_shifts: float32 [2, 2, 512], P(None, None, 'dp')
- grad_first: float32 [2, 8, 512, 2048], P(None, 'expert', None, 'dp')
- grad_second: float32 [2, 8, 2048, 512], P(None, 'expert', 'dp')
The draws below stay inside these ranges and needn't reach their ends.
Inputs may be any that keep to these rules, and one draw needn't show every extreme that they name: `routes`: the two experts of a token differ. Among the 394 tokens of one device in one block, no expert is named by more than 147 tokens, a bound that some block reaches.
All inputs are finite; a program needn't handle non-finite values.
Results may differ from the reference program's by a relative error of at most 0.019.
Values may be sent and summed in bfloat16 or wider, within the bound.
No kernel may reach another device: no remote copies, remote signals or barrier semaphores. Data moves between devices by JAX's collectives and lax.ppermute only.
A program may use at most 192 MiB of HBM per device.

```python
import math
import jax
import jax.numpy as jnp
import numpy as np
from jax import lax

D = 512
HEADS = 8
HEAD_DIM = 64
FF = 2048
SEQ = 197
LAYERS = 2
IMG_DEV = 2
EXPERTS = 8
IMAGES = 64
TOK_DEV = 394
CAP = 147


def steps_of(own_key, extent, cuts, smallest, high):
    factor_of = 1.0
    for dim, parts in cuts:
        heights = jax.random.uniform(jax.random.fold_in(jax.random.fold_in(own_key, 6), dim), (parts,), jnp.float32, smallest / len(cuts), high / len(cuts))
        factor_of = factor_of * jnp.repeat(jnp.exp(heights), extent[dim] // parts).reshape((-1,) + (1,) * (len(extent) - 1 - dim))
    return factor_of


def deal_out(rng, own, number, rows, count, top, bound, skew):
    ranking = jax.random.permutation(rng, count)
    heavy_load, ordinary = load_shares(count, rows * top, bound, skew, True), load_shares(count, rows * top, bound, skew, False)
    places = jnp.arange(count)

    def named(tallies, turn):
        used = int((tallies > 0).sum())
        fixed = max(1, used // 4)
        moved = fixed + (places - fixed + turn * (used - fixed)) % max(1, count - fixed)
        return jnp.zeros((count,), jnp.int32).at[ranking[jnp.where(places < fixed, places, moved)]].set(jnp.asarray(tallies, jnp.int32))

    tallies = jnp.where(number % 4 == 0, named(heavy_load, number // 4), named(ordinary, number - number // 4 - 1))
    mixed = jax.random.permutation(jax.random.fold_in(own, 3), count)
    donor, sink = mixed[0:count // 2 * 2:2], mixed[1:count // 2 * 2:2]
    margin = jnp.minimum(tallies[donor] - 1, bound - tallies[sink]) // 2
    margin = jnp.where((donor == ranking[0]) | (sink == ranking[0]) | (tallies[sink] == 0), 0, jnp.maximum(margin, 0))
    moved = jax.random.randint(jax.random.fold_in(own, 4), (count // 2,), 0, 1 << 20) % (margin + 1)
    tallies = tallies.at[donor].add(-moved).at[sink].add(moved)
    items = jnp.searchsorted(jnp.cumsum(tallies), jnp.arange(rows * top), side="right").astype(jnp.int32)
    table = items.reshape(top, rows).T
    table = table[jax.random.permutation(jax.random.fold_in(own, 1), rows)]
    turn = jax.random.randint(jax.random.fold_in(own, 2), (rows, 1), 0, top)
    return jnp.take_along_axis(table, (jnp.arange(top)[None, :] + turn) % top, axis=1)


def load_shares(amount, total, bound, slope, full):
    loads = [(1 << 20) // math.isqrt(standing ** slope) + 1 for standing in range(1, amount + 1)]
    largest = bound if full else min(bound, max(-(-total // amount), total * loads[0] // sum(loads)))
    least = 1 if total - largest >= amount - 1 else 0
    holding, surplus = [largest] + [least] * (amount - 1), total - largest - least * (amount - 1)
    while surplus > 0:
        movable = [i for i in range(1, amount) if holding[i] < largest] or [i for i in range(1, amount) if holding[i] < bound]
        mass, remaining = sum([loads[i] for i in movable]), surplus
        for i in movable:
            addition = min(bound - holding[i], max(1, remaining * loads[i] // mass), surplus)
            holding[i] = holding[i] + addition
            surplus = surplus - addition
    return np.array(holding)


def scatter_about(own_key, extent, deviation, most, cuts=(), kind=jnp.bfloat16):
    values = deviation * jax.random.normal(own_key, extent, jnp.float32)
    if cuts:
        values = values * steps_of(own_key, extent, cuts, -0.22, 0.18)
    return jnp.clip(values, -most, most).astype(kind)


def setup_inputs(seed: int = 0) -> dict:
    seeds = jax.random.split(jax.random.key(seed), 11)
    embedded = scatter_about(seeds[0], (IMAGES, SEQ, D), 1.0, 6.0, ((0, 32),))
    cotangent = scatter_about(seeds[1], (IMAGES, SEQ, D), 1.0, 6.0, ((0, 32),))
    w_qkv = scatter_about(seeds[2], (LAYERS, D, 3 * D), D ** -0.5, 0.25, ((1, 8),))
    w_proj = scatter_about(seeds[3], (LAYERS, D, D), (max(1, 2 * D // SEQ)) ** -0.5, 2.5, ((1, 8),))
    w_router = scatter_about(seeds[4], (LAYERS, D, EXPERTS), (2 * D) ** -0.5, 0.1875, ((1, 8),))
    norm_gains = jnp.clip(1.0 + 0.15 * jax.random.normal(seeds[5], (LAYERS, 2, D), jnp.float32), 0.25, 1.75).astype(jnp.bfloat16)
    norm_shifts = scatter_about(seeds[6], (LAYERS, 2, D), 0.2, 1.0, ((2, 8),))
    w_first = scatter_about(seeds[7], (LAYERS, EXPERTS, D, FF), D ** -0.5, 0.25, ((1, 4), (3, 8)))
    w_second = scatter_about(seeds[8], (LAYERS, EXPERTS, FF, D), (max(1, FF // (EXPERTS * EXPERTS))) ** -0.5, 1.0, ((1, 4), (2, 8)))
    routes_keys = jax.random.split(jax.random.fold_in(seeds[9], 1), LAYERS * IMAGES * SEQ // TOK_DEV)
    routes_turns = jax.random.permutation(jax.random.fold_in(seeds[9], 3), LAYERS * IMAGES * SEQ // TOK_DEV)
    routes = jax.vmap(lambda own, number: deal_out(jax.random.fold_in(seeds[9], 2), own, number, TOK_DEV, EXPERTS, 2, CAP, 1))(routes_keys, routes_turns).reshape((LAYERS, IMAGES, SEQ, 2))
    return {"embedded": embedded, "cotangent": cotangent, "w_qkv": w_qkv, "w_proj": w_proj, "w_router": w_router, "norm_gains": norm_gains, "norm_shifts": norm_shifts, "w_first": w_first, "w_second": w_second, "routes": routes}


@jax.custom_vjp
def low(v):
    return lax.optimization_barrier(v.astype(jnp.bfloat16)).astype(jnp.float32)

@jax.custom_vjp
def low_back(v):
    return v

def low_keep(v):
    return (low(v), None)

def low_pass(kept, grad):
    return (grad,)

def back_keep(v):
    return (v, None)

def back_low(kept, grad):
    return (low(grad),)
low.defvjp(low_keep, low_pass)
low_back.defvjp(back_keep, back_low)
EPSILON = 1e-06
ROOT_HALF = 0.7071067811865476
HIGHEST = lax.Precision.HIGHEST

def product(left, right):
    return jnp.dot(left, right, precision=HIGHEST)

def layer_norm(values, scale_in, shift_in):
    center = values - lax.optimization_barrier(jnp.mean(values, axis=-1, keepdims=True))
    variance = lax.optimization_barrier(jnp.mean(center * center, axis=-1, keepdims=True))
    return center * lax.rsqrt(variance + EPSILON) * scale_in + shift_in

def softmax_rows(scores):
    highest = lax.optimization_barrier(jnp.max(scores, axis=-1, keepdims=True))
    powers = jnp.exp(scores - highest)
    return powers / lax.optimization_barrier(jnp.sum(powers, axis=-1, keepdims=True))

def attend_group(query, keyed, valued):
    scores = low_back(jnp.einsum('gqhd,gkhd->ghqk', query, keyed, precision=HIGHEST))
    probs = low(softmax_rows(scores))
    return jnp.einsum('ghqk,gkhd->gqhd', probs, valued, precision=HIGHEST)

def expert_apply(blocks):
    rows_in, first, second = blocks
    preact = low_back(product(rows_in, first))
    hidden = low(0.5 * preact * (1.0 + lax.erf(preact * ROOT_HALF)))
    return low(low_back(product(hidden, second)))

def one_layer(resid, w_qkv, w_proj, w_router, gains, shifts, w_first, w_second, route):
    group_rows, width = resid.shape
    images = group_rows // SEQ
    attn_in = low(layer_norm(resid, gains[0], shifts[0]))
    packed = product(attn_in, w_qkv)
    query = low(low_back(packed[:, :width] * HEAD_DIM ** (-0.5)))
    keyed = low(low_back(packed[:, width:2 * width]))
    valued = low(low_back(packed[:, 2 * width:]))

    def split_heads(block):
        return block.reshape(images, SEQ, HEADS, HEAD_DIM)
    mixed = jax.checkpoint(attend_group)(split_heads(query), split_heads(keyed), split_heads(valued))
    mixed = low(low_back(mixed.reshape(group_rows, width)))
    resid_mid = resid + low_back(product(mixed, w_proj))
    moe_in = low(layer_norm(resid_mid, gains[1], shifts[1]))
    logits = low_back(product(moe_in, w_router))
    router_probs = softmax_rows(logits)
    gates = jnp.take_along_axis(router_probs, route, axis=1)
    experts_total = w_router.shape[1]
    pair_expert = route.reshape(-1)
    labels = jnp.arange(experts_total, dtype=jnp.int32)
    table = (pair_expert[:, None] == labels[None, :]).astype(jnp.int32)
    order = lax.optimization_barrier(jnp.sum((jnp.cumsum(table, axis=0) - 1) * table, axis=1)).astype(jnp.int32)
    per_expert = images // IMG_DEV * CAP
    pairs_in = jnp.repeat(moe_in, 2, axis=0)
    buffer = jnp.zeros((experts_total, per_expert, width), jnp.float32).at[pair_expert, order].set(pairs_in)
    buffer = low_back(buffer)
    outputs = lax.map(jax.checkpoint(expert_apply), (buffer, w_first, w_second))
    returned = outputs[pair_expert, order].reshape(group_rows, 2, width)
    return resid_mid + lax.optimization_barrier(jnp.sum(gates[:, :, None] * returned, axis=1))

def forward(images_in, params, route_block):
    w_qkv, w_proj, w_router, gains, shifts, w_first, w_second = params
    resid = images_in.reshape(-1, D)
    for which in range(LAYERS):
        resid = jax.checkpoint(one_layer)(resid, w_qkv[which], w_proj[which], w_router[which], gains[which], shifts[which], w_first[which], w_second[which], route_block[which])
    return resid

def reference(embedded, cotangent, w_qkv, w_proj, w_router, norm_gains, norm_shifts, w_first, w_second, routes):
    weights = tuple((tensor.astype(jnp.float32) for tensor in (w_qkv, w_proj, w_router, norm_gains, norm_shifts, w_first, w_second)))
    per_group = 16
    groups = IMAGES // per_group
    image_blocks = embedded.astype(jnp.float32).reshape(groups, per_group, SEQ, D)
    cot_blocks = cotangent.astype(jnp.float32).reshape(groups, per_group * SEQ, D)
    route_blocks = jnp.moveaxis(routes.reshape(LAYERS, groups, per_group * SEQ, 2), 1, 0)

    def step(totals, blocks):
        image_block, cot_block, route_block = blocks

        def closed(images_in, params):
            return forward(images_in, params, route_block)
        result, pull = jax.vjp(closed, image_block, weights)
        grad_in, grad_params = pull(cot_block)
        summed = tuple((old + new for old, new in zip(totals, grad_params)))
        return (summed, (result.astype(jnp.bfloat16), grad_in))
    initial = tuple((jnp.zeros(tensor.shape, jnp.float32) for tensor in weights))
    totals, (outputs, grads_in) = lax.scan(step, initial, (image_blocks, cot_blocks, route_blocks))
    out_images = outputs.reshape(IMAGES, SEQ, D)
    grad_images = grads_in.reshape(IMAGES, SEQ, D)
    return (out_images, grad_images, totals[0], totals[1], totals[2], totals[3], totals[4], totals[5], totals[6])
```

```python
import jax
import jax.numpy as jnp
from jax import lax
from jax.sharding import PartitionSpec as P

HEADS = 8
HEAD_DIM = 64
SEQ = 197
LAYERS = 2


EPSILON = 1e-06
ROOT_HALF = 0.7071067811865476
INV_ROOT_TAU = 0.3989422804014327


def layer_norm(values, scale_in, shift_in):
    center = values - jnp.mean(values, axis=-1, keepdims=True)
    variance = jnp.mean(center * center, axis=-1, keepdims=True)
    inverse = lax.rsqrt(variance + EPSILON)
    normed = center * inverse
    return (normed * scale_in + shift_in, normed, inverse)


def norm_back(grad_out, normed, inverse, scale_in):
    grad_normed = grad_out * scale_in
    first_mean = jnp.mean(grad_normed, axis=-1, keepdims=True)
    second_mean = jnp.mean(grad_normed * normed, axis=-1, keepdims=True)
    grad_in = inverse * (grad_normed - first_mean - normed * second_mean)
    return (grad_in, jnp.sum(grad_out * normed, axis=0), jnp.sum(grad_out, axis=0))


def softmax_rows(scores):
    highest = jnp.max(scores, axis=-1, keepdims=True)
    powers = jnp.exp(scores - highest)
    row_total = jnp.sum(powers, axis=-1, keepdims=True)
    return (powers / row_total, highest + jnp.log(row_total))


def gelu_value(preact):
    return 0.5 * preact * (1.0 + lax.erf(preact * ROOT_HALF))


def gelu_slope(preact):
    return (
        0.5 * (1.0 + lax.erf(preact * ROOT_HALF))
        + preact * jnp.exp(-0.5 * preact * preact) * INV_ROOT_TAU
    )


def gather_dense(which, w_qkv, w_proj, w_router, norm_gains, norm_shifts):
    packed = jnp.concatenate(
        [
            w_qkv[which],
            w_proj[which],
            w_router[which],
            norm_gains[which].T,
            norm_shifts[which].T,
        ],
        axis=1,
    )
    full = lax.all_gather(packed, "dp", axis=0, tiled=True)
    width = full.shape[0]
    experts = w_router.shape[2]
    wide = full[:, 4 * width :]
    gains = wide[:, experts : experts + 2].T.astype(jnp.float32)
    shifts = wide[:, experts + 2 : experts + 4].T.astype(jnp.float32)
    return (full[:, : 3 * width], full[:, 3 * width : 4 * width], wide[:, :experts], gains, shifts)


def gather_experts(which, w_first, w_second):
    first_full = lax.all_gather(w_first[which], "dp", axis=2, tiled=True)
    second_full = lax.all_gather(w_second[which], "dp", axis=1, tiled=True)
    return (first_full, second_full)


def route_tables(route, experts_total, capacity):
    labels = jnp.arange(experts_total, dtype=jnp.int32)
    pick_first = (route[:, 0:1] == labels[None, :]).astype(jnp.int32)
    pick_second = (route[:, 1:2] == labels[None, :]).astype(jnp.int32)
    both_picks = pick_first + pick_second
    before = jnp.cumsum(both_picks, axis=0) - both_picks
    slot_first = route[:, 0] * capacity + jnp.sum(before * pick_first, axis=1)
    slot_second = route[:, 1] * capacity + jnp.sum(before * pick_second, axis=1)
    slot_ids = jnp.arange(experts_total * capacity, dtype=jnp.int32)
    place_first = (slot_ids[:, None] == slot_first[None, :]).astype(jnp.bfloat16)
    place_second = (slot_ids[:, None] == slot_second[None, :]).astype(jnp.bfloat16)
    return (
        pick_first.astype(jnp.float32),
        pick_second.astype(jnp.float32),
        place_first,
        place_second,
    )


def exchange(block):
    return lax.all_to_all(block, "expert", split_axis=0, concat_axis=0, tiled=True)


def layer_forward(resid, dense, experts, tables):
    qkv_full, proj_full, router_full, gains_wide, shifts_wide = dense
    first_full, second_full = experts
    pick_first_f, pick_second_f, place_first, place_second = tables
    tok_count, width = resid.shape
    images = tok_count // SEQ
    attn_norm, unit_a, inv_a = layer_norm(resid, gains_wide[0], shifts_wide[0])
    attn_in = attn_norm.astype(jnp.bfloat16)
    packed = jnp.dot(attn_in, qkv_full, preferred_element_type=jnp.float32)
    head_shape = (images, SEQ, HEADS, HEAD_DIM)
    query = (packed[:, :width] * HEAD_DIM ** (-0.5)).astype(jnp.bfloat16).reshape(head_shape)
    keyed = packed[:, width : 2 * width].astype(jnp.bfloat16).reshape(head_shape)
    valued = packed[:, 2 * width :].astype(jnp.bfloat16).reshape(head_shape)
    scores = jnp.einsum("iqhd,ikhd->ihqk", query, keyed, preferred_element_type=jnp.float32)
    probs, log_total = softmax_rows(scores)
    mixed = jnp.einsum(
        "ihqk,ikhd->iqhd", probs.astype(jnp.bfloat16), valued, preferred_element_type=jnp.float32
    )
    mixed = mixed.reshape(tok_count, width).astype(jnp.bfloat16)
    resid_mid = resid + jnp.dot(mixed, proj_full, preferred_element_type=jnp.float32)
    moe_norm, unit_b, inv_b = layer_norm(resid_mid, gains_wide[1], shifts_wide[1])
    moe_in = moe_norm.astype(jnp.bfloat16)
    logits = jnp.dot(moe_in, router_full, preferred_element_type=jnp.float32)
    router_probs, _ = softmax_rows(logits)
    experts_total = router_full.shape[1]
    local_count = first_full.shape[0]
    peers = lax.axis_size("expert")
    capacity = place_first.shape[0] // experts_total
    outgoing = jnp.dot(place_first + place_second, moe_in, preferred_element_type=jnp.float32)
    outgoing = outgoing.astype(jnp.bfloat16).reshape(peers, local_count, capacity, width)
    incoming = exchange(outgoing)
    hidden_pre = jnp.einsum(
        "sjcd,jdf->sjcf", incoming, first_full, preferred_element_type=jnp.float32
    )
    hidden_act = gelu_value(hidden_pre).astype(jnp.bfloat16)
    result = jnp.einsum(
        "sjcf,jfd->sjcd", hidden_act, second_full, preferred_element_type=jnp.float32
    ).astype(jnp.bfloat16)
    returned = exchange(result).reshape(experts_total * capacity, width)
    gate_first = jnp.sum(router_probs * pick_first_f, axis=1)
    gate_second = jnp.sum(router_probs * pick_second_f, axis=1)
    back_first = jnp.einsum("st,sd->td", place_first, returned, preferred_element_type=jnp.float32)
    back_second = jnp.einsum(
        "st,sd->td", place_second, returned, preferred_element_type=jnp.float32
    )
    resid_out = resid_mid + (gate_first[:, None] * back_first + gate_second[:, None] * back_second)
    saved = (
        unit_a,
        inv_a,
        attn_in,
        query,
        keyed,
        valued,
        log_total,
        mixed,
        unit_b,
        inv_b,
        moe_in,
        router_probs,
        incoming,
        hidden_pre,
        hidden_act,
        back_first,
        back_second,
        gate_first,
        gate_second,
    )
    return (resid_out, saved)


def layer_backward(grad_out, dense, experts, tables, saved):
    qkv_full, proj_full, router_full, gains_wide, _ = dense
    first_full, second_full = experts
    pick_first_f, pick_second_f, place_first, place_second = tables
    (
        unit_a,
        inv_a,
        attn_in,
        query,
        keyed,
        valued,
        log_total,
        mixed,
        unit_b,
        inv_b,
        moe_in,
        router_probs,
        incoming,
        hidden_pre,
        hidden_act,
        back_first,
        back_second,
        gate_first,
        gate_second,
    ) = saved
    tok_count, width = grad_out.shape
    images = tok_count // SEQ
    send_first = (gate_first[:, None] * grad_out).astype(jnp.bfloat16)
    send_second = (gate_second[:, None] * grad_out).astype(jnp.bfloat16)
    slot_grads = jnp.dot(place_first, send_first, preferred_element_type=jnp.float32) + jnp.dot(
        place_second, send_second, preferred_element_type=jnp.float32
    )
    slot_grads = slot_grads.astype(jnp.bfloat16).reshape(incoming.shape)
    grad_result = exchange(slot_grads)
    grad_gate_first = jnp.sum(grad_out * back_first, axis=1)
    grad_gate_second = jnp.sum(grad_out * back_second, axis=1)
    grad_act = jnp.einsum(
        "sjcd,jfd->sjcf", grad_result, second_full, preferred_element_type=jnp.float32
    )
    grad_pre = (grad_act * gelu_slope(hidden_pre)).astype(jnp.bfloat16)
    grad_rows = jnp.einsum(
        "sjcf,jdf->sjcd", grad_pre, first_full, preferred_element_type=jnp.float32
    ).astype(jnp.bfloat16)
    grad_back = exchange(grad_rows)
    grad_second = jnp.einsum(
        "sjcf,sjcd->jfd", hidden_act, grad_result, preferred_element_type=jnp.float32
    ).astype(jnp.bfloat16)
    grad_first = jnp.einsum(
        "sjcd,sjcf->jdf", incoming, grad_pre, preferred_element_type=jnp.float32
    ).astype(jnp.bfloat16)
    grad_back, grad_second, grad_first = lax.optimization_barrier(
        (grad_back, grad_second, grad_first)
    )
    share_second = lax.psum_scatter(grad_second, "dp", scatter_dimension=1, tiled=True)
    share_first = lax.psum_scatter(grad_first, "dp", scatter_dimension=2, tiled=True)
    grad_back = grad_back.reshape(-1, width)
    grad_moe = jnp.einsum(
        "st,sd->td", place_first + place_second, grad_back, preferred_element_type=jnp.float32
    )
    grad_probs = pick_first_f * grad_gate_first[:, None] + pick_second_f * grad_gate_second[:, None]
    weighted = jnp.sum(router_probs * grad_probs, axis=1, keepdims=True)
    grad_logits = (router_probs * (grad_probs - weighted)).astype(jnp.bfloat16)
    grad_router = jnp.einsum("td,te->de", moe_in, grad_logits, preferred_element_type=jnp.float32)
    grad_moe = grad_moe + jnp.einsum(
        "te,de->td", grad_logits, router_full, preferred_element_type=jnp.float32
    )
    grad_norm_b, gain_b_grad, shift_b_grad = norm_back(grad_moe, unit_b, inv_b, gains_wide[1])
    grad_mid = grad_out + grad_norm_b
    grad_branch = grad_mid.astype(jnp.bfloat16)
    grad_proj = jnp.einsum("td,te->de", mixed, grad_branch, preferred_element_type=jnp.float32)
    grad_mixed = jnp.einsum("te,de->td", grad_branch, proj_full, preferred_element_type=jnp.float32)
    grad_mixed = grad_mixed.astype(jnp.bfloat16).reshape(images, SEQ, HEADS, HEAD_DIM)
    scores = jnp.einsum("iqhd,ikhd->ihqk", query, keyed, preferred_element_type=jnp.float32)
    probs = jnp.exp(scores - log_total)
    grad_weights = jnp.einsum(
        "iqhd,ikhd->ihqk", grad_mixed, valued, preferred_element_type=jnp.float32
    )
    grad_valued = jnp.einsum(
        "ihqk,iqhd->ikhd",
        probs.astype(jnp.bfloat16),
        grad_mixed,
        preferred_element_type=jnp.float32,
    ).astype(jnp.bfloat16)
    row_inner = jnp.sum(probs * grad_weights, axis=-1, keepdims=True)
    grad_scores = (probs * (grad_weights - row_inner)).astype(jnp.bfloat16)
    grad_query = jnp.einsum(
        "ihqk,ikhd->iqhd", grad_scores, keyed, preferred_element_type=jnp.float32
    ).astype(jnp.bfloat16)
    grad_query = grad_query * jnp.asarray(HEAD_DIM ** (-0.5), jnp.bfloat16)
    grad_keyed = jnp.einsum(
        "ihqk,iqhd->ikhd", grad_scores, query, preferred_element_type=jnp.float32
    ).astype(jnp.bfloat16)
    grad_packed = jnp.concatenate(
        [
            grad_query.reshape(tok_count, width),
            grad_keyed.reshape(tok_count, width),
            grad_valued.reshape(tok_count, width),
        ],
        axis=1,
    )
    grad_qkv = jnp.einsum("td,te->de", attn_in, grad_packed, preferred_element_type=jnp.float32)
    grad_attn = jnp.einsum("te,de->td", grad_packed, qkv_full, preferred_element_type=jnp.float32)
    grad_norm_a, gain_a_grad, shift_a_grad = norm_back(grad_attn, unit_a, inv_a, gains_wide[0])
    grad_in = grad_mid + grad_norm_a
    low = jnp.bfloat16
    small = jnp.concatenate(
        [
            grad_qkv.astype(low),
            grad_proj.astype(low),
            grad_router.astype(low),
            jnp.stack([gain_a_grad, gain_b_grad, shift_a_grad, shift_b_grad], axis=1).astype(low),
        ],
        axis=1,
    )
    share_small = lax.psum_scatter(small, "dp", scatter_dimension=0, tiled=True)
    return (grad_in, share_small, share_first, share_second)


def body(
    embedded, cotangent, w_qkv, w_proj, w_router, norm_gains, norm_shifts, w_first, w_second, routes
):
    images, length, width = embedded.shape
    tok_count = images * length
    experts_total = w_router.shape[2]
    capacity = -(-max(2, 3 * tok_count // experts_total) // 8) * 8
    resid = embedded.reshape(tok_count, width).astype(jnp.float32)
    dense, experts, tables, saved = [], [], [], []
    for which in range(LAYERS):
        dense.append(gather_dense(which, w_qkv, w_proj, w_router, norm_gains, norm_shifts))
        experts.append(gather_experts(which, w_first, w_second))
    for which in range(LAYERS):
        tables.append(route_tables(routes[which].reshape(tok_count, 2), experts_total, capacity))
        resid, kept = layer_forward(resid, dense[which], experts[which], tables[which])
        saved.append(kept)
    out_images = resid.reshape(images, length, width).astype(jnp.bfloat16)
    grad = cotangent.reshape(tok_count, width).astype(jnp.float32)
    smalls, firsts, seconds = [None] * LAYERS, [None] * LAYERS, [None] * LAYERS
    for which in reversed(range(LAYERS)):
        grad, smalls[which], firsts[which], seconds[which] = layer_backward(
            grad, dense[which], experts[which], tables[which], saved[which]
        )
    total = lax.psum(jnp.stack(smalls), "expert").astype(jnp.float32)
    grad_images = grad.reshape(images, length, width)
    wide = total[:, :, 4 * width :]
    return (
        out_images,
        grad_images,
        total[:, :, : 3 * width],
        total[:, :, 3 * width : 4 * width],
        wide[:, :, :experts_total],
        jnp.swapaxes(wide[:, :, experts_total : experts_total + 2], 1, 2),
        jnp.swapaxes(wide[:, :, experts_total + 2 :], 1, 2),
        jnp.stack(firsts).astype(jnp.float32),
        jnp.stack(seconds).astype(jnp.float32),
    )


def solution(mesh):
    return jax.shard_map(
        body,
        mesh=mesh,
        in_specs=(
            P(("dp", "expert"), None, None),
            P(("dp", "expert"), None, None),
            P(None, "dp", None),
            P(None, "dp", None),
            P(None, "dp", None),
            P(None, None, "dp"),
            P(None, None, "dp"),
            P(None, "expert", None, "dp"),
            P(None, "expert", "dp", None),
            P(None, ("dp", "expert"), None, None),
        ),
        out_specs=(
            P(("dp", "expert"), None, None),
            P(("dp", "expert"), None, None),
            P(None, "dp", None),
            P(None, "dp", None),
            P(None, "dp", None),
            P(None, None, "dp"),
            P(None, None, "dp"),
            P(None, "expert", None, "dp"),
            P(None, "expert", "dp", None),
        ),
        check_vma=False,
    )
```

```python
import jax
import jax.numpy as jnp
from jax import lax
from jax.sharding import PartitionSpec as P

HEADS = 8
HEAD_DIM = 64
SEQ = 197
LAYERS = 2


EPSILON = 1e-06
ROOT_HALF = 0.7071067811865476
INV_ROOT_TAU = 0.3989422804014327


def layer_norm(values, scale_in, shift_in):
    center = values - jnp.mean(values, axis=-1, keepdims=True)
    variance = jnp.mean(center * center, axis=-1, keepdims=True)
    inverse = lax.rsqrt(variance + EPSILON)
    normed = center * inverse
    return (normed * scale_in + shift_in, normed, inverse)


def norm_back(grad_out, normed, inverse, scale_in):
    grad_normed = grad_out * scale_in
    first_mean = jnp.mean(grad_normed, axis=-1, keepdims=True)
    second_mean = jnp.mean(grad_normed * normed, axis=-1, keepdims=True)
    grad_in = inverse * (grad_normed - first_mean - normed * second_mean)
    return (grad_in, jnp.sum(grad_out * normed, axis=0), jnp.sum(grad_out, axis=0))


def softmax_rows(scores):
    highest = jnp.max(scores, axis=-1, keepdims=True)
    powers = jnp.exp(scores - highest)
    row_total = jnp.sum(powers, axis=-1, keepdims=True)
    return (powers / row_total, highest + jnp.log(row_total))


def gelu_value(preact):
    return 0.5 * preact * (1.0 + lax.erf(preact * ROOT_HALF))


def gelu_slope(preact):
    return (
        0.5 * (1.0 + lax.erf(preact * ROOT_HALF))
        + preact * jnp.exp(-0.5 * preact * preact) * INV_ROOT_TAU
    )


def gather_dense(which, w_qkv, w_proj, w_router, norm_gains, norm_shifts):
    packed = jnp.concatenate(
        [
            w_qkv[which],
            w_proj[which],
            w_router[which],
            norm_gains[which].T,
            norm_shifts[which].T,
        ],
        axis=1,
    )
    full = lax.all_gather(packed, "dp", axis=0, tiled=True)
    width = full.shape[0]
    experts = w_router.shape[2]
    wide = full[:, 4 * width :]
    gains = wide[:, experts : experts + 2].T.astype(jnp.float32)
    shifts = wide[:, experts + 2 : experts + 4].T.astype(jnp.float32)
    return (full[:, : 3 * width], full[:, 3 * width : 4 * width], wide[:, :experts], gains, shifts)


def gather_experts(which, w_first, w_second):
    first_full = lax.all_gather(w_first[which], "dp", axis=2, tiled=True)
    second_full = lax.all_gather(w_second[which], "dp", axis=1, tiled=True)
    return (first_full, second_full)


def route_tables(route, experts_total, capacity):
    labels = jnp.arange(experts_total, dtype=jnp.int32)
    pick_first = (route[:, 0:1] == labels[None, :]).astype(jnp.int32)
    pick_second = (route[:, 1:2] == labels[None, :]).astype(jnp.int32)
    both_picks = pick_first + pick_second
    before = jnp.cumsum(both_picks, axis=0) - both_picks
    slot_first = route[:, 0] * capacity + jnp.sum(before * pick_first, axis=1)
    slot_second = route[:, 1] * capacity + jnp.sum(before * pick_second, axis=1)
    slot_ids = jnp.arange(experts_total * capacity, dtype=jnp.int32)
    place_first = (slot_ids[:, None] == slot_first[None, :]).astype(jnp.bfloat16)
    place_second = (slot_ids[:, None] == slot_second[None, :]).astype(jnp.bfloat16)
    return (
        pick_first.astype(jnp.float32),
        pick_second.astype(jnp.float32),
        place_first,
        place_second,
    )


def exchange(block):
    return lax.all_to_all(block, "expert", split_axis=0, concat_axis=0, tiled=True)


def attend_forward(resid, dense, tables):
    qkv_full, proj_full, router_full, gains_wide, shifts_wide = dense
    pick_first_f, pick_second_f, _, _ = tables
    tok_count, width = resid.shape
    images = tok_count // SEQ
    attn_norm, unit_a, inv_a = layer_norm(resid, gains_wide[0], shifts_wide[0])
    attn_in = attn_norm.astype(jnp.bfloat16)
    packed = jnp.dot(attn_in, qkv_full, preferred_element_type=jnp.float32)
    head_shape = (images, SEQ, HEADS, HEAD_DIM)
    query = (packed[:, :width] * HEAD_DIM ** (-0.5)).astype(jnp.bfloat16).reshape(head_shape)
    keyed = packed[:, width : 2 * width].astype(jnp.bfloat16).reshape(head_shape)
    valued = packed[:, 2 * width :].astype(jnp.bfloat16).reshape(head_shape)
    scores = jnp.einsum("iqhd,ikhd->ihqk", query, keyed, preferred_element_type=jnp.float32)
    probs, log_total = softmax_rows(scores)
    mixed = jnp.einsum(
        "ihqk,ikhd->iqhd", probs.astype(jnp.bfloat16), valued, preferred_element_type=jnp.float32
    )
    mixed = mixed.reshape(tok_count, width).astype(jnp.bfloat16)
    resid_mid = resid + jnp.dot(mixed, proj_full, preferred_element_type=jnp.float32)
    moe_norm, unit_b, inv_b = layer_norm(resid_mid, gains_wide[1], shifts_wide[1])
    moe_in = moe_norm.astype(jnp.bfloat16)
    logits = jnp.dot(moe_in, router_full, preferred_element_type=jnp.float32)
    router_probs, _ = softmax_rows(logits)
    gate_first = jnp.sum(router_probs * pick_first_f, axis=1)
    gate_second = jnp.sum(router_probs * pick_second_f, axis=1)
    router_probs, gate_first, gate_second = lax.optimization_barrier(
        (router_probs, gate_first, gate_second)
    )
    attn_saved = (unit_a, inv_a, attn_in, query, keyed, valued, log_total, mixed)
    moe_saved = (unit_b, inv_b, moe_in, router_probs, gate_first, gate_second)
    return (resid_mid, attn_saved, moe_saved)


def slots_of(rows, place, block_shape):
    slots = jnp.dot(place, rows, preferred_element_type=jnp.float32)
    return slots.astype(jnp.bfloat16).reshape(block_shape)


def gated_slots(grad_out, moe_saved, tables, block_shape):
    gate_first, gate_second = moe_saved[4:]
    place_first, place_second = tables[2:]
    send_first = (gate_first[:, None] * grad_out).astype(jnp.bfloat16)
    send_second = (gate_second[:, None] * grad_out).astype(jnp.bfloat16)
    slots = jnp.dot(place_first, send_first, preferred_element_type=jnp.float32) + jnp.dot(
        place_second, send_second, preferred_element_type=jnp.float32
    )
    return slots.astype(jnp.bfloat16).reshape(block_shape)


def experts_hidden(incoming, first_full):
    hidden_pre = jnp.einsum(
        "sjcd,jdf->sjcf", incoming, first_full, preferred_element_type=jnp.float32
    )
    return (hidden_pre, gelu_value(hidden_pre).astype(jnp.bfloat16))


def experts_result(hidden_act, second_full):
    return jnp.einsum(
        "sjcf,jfd->sjcd", hidden_act, second_full, preferred_element_type=jnp.float32
    ).astype(jnp.bfloat16)


def rows_back(returned, place):
    return jnp.einsum("st,sd->td", place, returned, preferred_element_type=jnp.float32)


def experts_backward(grad_result, incoming, hidden_pre, hidden_act, experts):
    first_full, second_full = experts
    grad_second = jnp.einsum(
        "sjcf,sjcd->jfd", hidden_act, grad_result, preferred_element_type=jnp.float32
    ).astype(jnp.bfloat16)
    share_second = lax.psum_scatter(grad_second, "dp", scatter_dimension=1, tiled=True)
    grad_act = jnp.einsum(
        "sjcd,jfd->sjcf", grad_result, second_full, preferred_element_type=jnp.float32
    )
    grad_pre = (grad_act * gelu_slope(hidden_pre)).astype(jnp.bfloat16)
    grad_rows = jnp.einsum(
        "sjcf,jdf->sjcd", grad_pre, first_full, preferred_element_type=jnp.float32
    ).astype(jnp.bfloat16)
    grad_back = exchange(grad_rows)
    grad_first = jnp.einsum(
        "sjcd,sjcf->jdf", incoming, grad_pre, preferred_element_type=jnp.float32
    ).astype(jnp.bfloat16)
    grad_back, grad_first = lax.optimization_barrier((grad_back, grad_first))
    share_first = lax.psum_scatter(grad_first, "dp", scatter_dimension=2, tiled=True)
    return (grad_back, share_first, share_second)


def tokens_backward(grad_out, grad_back, backs, dense, tables, attn_saved, moe_saved):
    qkv_full, proj_full, router_full, gains_wide, _ = dense
    pick_first_f, pick_second_f, place_first, place_second = tables
    unit_a, inv_a, attn_in, query, keyed, valued, log_total, mixed = attn_saved
    unit_b, inv_b, moe_in, router_probs, _, _ = moe_saved
    tok_count, width = grad_out.shape
    images = tok_count // SEQ
    grad_gate_first = jnp.sum(grad_out * backs[0], axis=1)
    grad_gate_second = jnp.sum(grad_out * backs[1], axis=1)
    grad_back = grad_back.reshape(-1, width)
    grad_moe = rows_back(grad_back, place_first + place_second)
    grad_probs = pick_first_f * grad_gate_first[:, None] + pick_second_f * grad_gate_second[:, None]
    weighted = jnp.sum(router_probs * grad_probs, axis=1, keepdims=True)
    grad_logits = (router_probs * (grad_probs - weighted)).astype(jnp.bfloat16)
    grad_router = jnp.einsum("td,te->de", moe_in, grad_logits, preferred_element_type=jnp.float32)
    grad_moe = grad_moe + jnp.einsum(
        "te,de->td", grad_logits, router_full, preferred_element_type=jnp.float32
    )
    grad_norm_b, gain_b_grad, shift_b_grad = norm_back(grad_moe, unit_b, inv_b, gains_wide[1])
    grad_mid = grad_out + grad_norm_b
    grad_branch = grad_mid.astype(jnp.bfloat16)
    grad_proj = jnp.einsum("td,te->de", mixed, grad_branch, preferred_element_type=jnp.float32)
    grad_mixed = jnp.einsum("te,de->td", grad_branch, proj_full, preferred_element_type=jnp.float32)
    grad_mixed = grad_mixed.astype(jnp.bfloat16).reshape(images, SEQ, HEADS, HEAD_DIM)
    scores = jnp.einsum("iqhd,ikhd->ihqk", query, keyed, preferred_element_type=jnp.float32)
    probs = jnp.exp(scores - log_total)
    grad_weights = jnp.einsum(
        "iqhd,ikhd->ihqk", grad_mixed, valued, preferred_element_type=jnp.float32
    )
    grad_valued = jnp.einsum(
        "ihqk,iqhd->ikhd",
        probs.astype(jnp.bfloat16),
        grad_mixed,
        preferred_element_type=jnp.float32,
    ).astype(jnp.bfloat16)
    row_inner = jnp.sum(probs * grad_weights, axis=-1, keepdims=True)
    grad_scores = (probs * (grad_weights - row_inner)).astype(jnp.bfloat16)
    grad_query = jnp.einsum(
        "ihqk,ikhd->iqhd", grad_scores, keyed, preferred_element_type=jnp.float32
    ).astype(jnp.bfloat16)
    grad_query = grad_query * jnp.asarray(HEAD_DIM ** (-0.5), jnp.bfloat16)
    grad_keyed = jnp.einsum(
        "ihqk,iqhd->ikhd", grad_scores, query, preferred_element_type=jnp.float32
    ).astype(jnp.bfloat16)
    grad_packed = jnp.concatenate(
        [
            grad_query.reshape(tok_count, width),
            grad_keyed.reshape(tok_count, width),
            grad_valued.reshape(tok_count, width),
        ],
        axis=1,
    )
    grad_qkv = jnp.einsum("td,te->de", attn_in, grad_packed, preferred_element_type=jnp.float32)
    grad_attn = jnp.einsum("te,de->td", grad_packed, qkv_full, preferred_element_type=jnp.float32)
    grad_norm_a, gain_a_grad, shift_a_grad = norm_back(grad_attn, unit_a, inv_a, gains_wide[0])
    grad_in = grad_mid + grad_norm_a
    low = jnp.bfloat16
    small = jnp.concatenate(
        [
            grad_qkv.astype(low),
            grad_proj.astype(low),
            grad_router.astype(low),
            jnp.stack([gain_a_grad, gain_b_grad, shift_a_grad, shift_b_grad], axis=1).astype(low),
        ],
        axis=1,
    )
    peers, shares = lax.axis_size("expert"), lax.axis_size("dp")
    piece = width // (peers * shares)
    columns = small.shape[1]
    small = small.reshape(shares, peers, piece, columns).swapaxes(0, 1)
    small = exchange(small)
    small = jnp.sum(small.astype(jnp.float32), axis=0).astype(low)
    return (grad_in, small)


def whole_step(
    embedded, cotangent, w_qkv, w_proj, w_router, norm_gains, norm_shifts, w_first, w_second, routes
):
    images, length, width = embedded.shape
    tok_count = images * length
    experts_total = w_router.shape[2]
    peers = lax.axis_size("expert")
    capacity = -(-max(2, 3 * tok_count // experts_total) // 8) * 8
    block_shape = (peers, experts_total // peers, capacity, width)
    resid = embedded.reshape(tok_count, width).astype(jnp.float32)
    grad = cotangent.reshape(tok_count, width).astype(jnp.float32)
    dense, experts, tables = [], [], []
    for which in range(LAYERS):
        dense.append(gather_dense(which, w_qkv, w_proj, w_router, norm_gains, norm_shifts))
        experts.append(gather_experts(which, w_first, w_second))
    attn_saved, moe_saved, kept = [], [], []
    grad_result = None
    for which in range(LAYERS):
        table = route_tables(routes[which].reshape(tok_count, 2), experts_total, capacity)
        tables.append(table)
        resid_mid, attn_part, moe_part = attend_forward(resid, dense[which], table)
        outgoing = slots_of(moe_part[2], table[2] + table[3], block_shape)
        incoming = exchange(outgoing)
        if which == LAYERS - 1:
            slots = gated_slots(grad, moe_part, table, block_shape)
            grad_result = exchange(slots)
        hidden_pre, hidden_act = experts_hidden(incoming, experts[which][0])
        result = experts_result(hidden_act, experts[which][1])
        returned = exchange(result).reshape(experts_total * capacity, width)
        backs = (rows_back(returned, table[2]), rows_back(returned, table[3]))
        resid = resid_mid + (
            moe_part[4][:, None] * backs[0] + moe_part[5][:, None] * backs[1]
        )
        attn_saved.append(attn_part)
        moe_saved.append(moe_part)
        kept.append((incoming, hidden_pre, hidden_act, backs))
    out_images = resid.reshape(images, length, width).astype(jnp.bfloat16)
    smalls, firsts, seconds = [None] * LAYERS, [None] * LAYERS, [None] * LAYERS
    for which in reversed(range(LAYERS)):
        incoming, hidden_pre, hidden_act, backs = kept[which]
        if which < LAYERS - 1:
            slots = gated_slots(grad, moe_saved[which], tables[which], block_shape)
            grad_result = exchange(slots)
        grad_back, firsts[which], seconds[which] = experts_backward(
            grad_result, incoming, hidden_pre, hidden_act, experts[which]
        )
        grad, smalls[which] = tokens_backward(
            grad,
            grad_back,
            backs,
            dense[which],
            tables[which],
            attn_saved[which],
            moe_saved[which],
        )
    both = jnp.stack(smalls, axis=2)
    both = lax.psum_scatter(both, "dp", scatter_dimension=0, tiled=True)[0]
    total = lax.all_gather(both, "expert", axis=0, tiled=True)
    total = total.swapaxes(0, 1).astype(jnp.float32)
    grad_images = grad.reshape(images, length, width)
    wide = total[:, :, 4 * width :]
    return (
        out_images,
        grad_images,
        total[:, :, : 3 * width],
        total[:, :, 3 * width : 4 * width],
        wide[:, :, :experts_total],
        jnp.swapaxes(wide[:, :, experts_total : experts_total + 2], 1, 2),
        jnp.swapaxes(wide[:, :, experts_total + 2 :], 1, 2),
        jnp.stack(firsts).astype(jnp.float32),
        jnp.stack(seconds).astype(jnp.float32),
    )


def solution(mesh):

    return jax.shard_map(
        whole_step,
        mesh=mesh,
        in_specs=(
            P(("dp", "expert"), None, None),
            P(("dp", "expert"), None, None),
            P(None, "dp", None),
            P(None, "dp", None),
            P(None, "dp", None),
            P(None, None, "dp"),
            P(None, None, "dp"),
            P(None, "expert", None, "dp"),
            P(None, "expert", "dp", None),
            P(None, ("dp", "expert"), None, None),
        ),
        out_specs=(
            P(("dp", "expert"), None, None),
            P(("dp", "expert"), None, None),
            P(None, "dp", None),
            P(None, "dp", None),
            P(None, "dp", None),
            P(None, None, "dp"),
            P(None, None, "dp"),
            P(None, "expert", None, "dp"),
            P(None, "expert", "dp", None),
        ),
        check_vma=False,
    )
```

```python
import jax
import jax.numpy as jnp
from jax import lax
from jax.sharding import PartitionSpec as P

HEADS = 8
HEAD_DIM = 64
SEQ = 197
LAYERS = 2


EPSILON = 1e-06
ROOT_HALF = 0.7071067811865476
INV_ROOT_TAU = 0.3989422804014327


def layer_norm(values, scale_in, shift_in):
    center = values - jnp.mean(values, axis=-1, keepdims=True)
    variance = jnp.mean(center * center, axis=-1, keepdims=True)
    inverse = lax.rsqrt(variance + EPSILON)
    normed = center * inverse
    return (normed * scale_in + shift_in, normed, inverse)


def norm_back(grad_out, normed, inverse, scale_in):
    grad_normed = grad_out * scale_in
    first_mean = jnp.mean(grad_normed, axis=-1, keepdims=True)
    second_mean = jnp.mean(grad_normed * normed, axis=-1, keepdims=True)
    grad_in = inverse * (grad_normed - first_mean - normed * second_mean)
    return (grad_in, jnp.sum(grad_out * normed, axis=0), jnp.sum(grad_out, axis=0))


def softmax_rows(scores):
    highest = jnp.max(scores, axis=-1, keepdims=True)
    powers = jnp.exp(scores - highest)
    row_total = jnp.sum(powers, axis=-1, keepdims=True)
    return (powers / row_total, highest + jnp.log(row_total))


def gelu_value(preact):
    return 0.5 * preact * (1.0 + lax.erf(preact * ROOT_HALF))


def gelu_slope(preact):
    return (
        0.5 * (1.0 + lax.erf(preact * ROOT_HALF))
        + preact * jnp.exp(-0.5 * preact * preact) * INV_ROOT_TAU
    )


def gather_quarters(w_qkv, w_proj, w_router, norm_gains, norm_shifts):
    peers, rank = lax.axis_size("expert"), lax.axis_index("expert")
    piece = w_qkv.shape[1] // peers
    packed = jnp.concatenate(
        [w_qkv, w_proj, w_router, jnp.swapaxes(norm_gains, 1, 2), jnp.swapaxes(norm_shifts, 1, 2)],
        axis=2,
    )
    packed = lax.dynamic_slice_in_dim(packed, rank * piece, piece, axis=1)
    return lax.all_gather(packed, "dp", axis=1, tiled=True)


def spread_dense(quarter, experts):
    peers, shares = lax.axis_size("expert"), lax.axis_size("dp")
    rows, columns = quarter.shape
    parts = exchange(jnp.broadcast_to(quarter[None], (peers, rows, columns)))
    width = peers * rows
    parts = parts.reshape(peers, shares, rows // shares, columns)

    def whole(start, stop):
        return parts[..., start:stop].swapaxes(0, 1).reshape(width, stop - start)

    base = 4 * width
    wide = whole(base, columns)
    gains = wide[:, experts : experts + 2].T.astype(jnp.float32)
    shifts = wide[:, experts + 2 : experts + 4].T.astype(jnp.float32)
    return (whole(0, 3 * width), whole(3 * width, base), wide[:, :experts], gains, shifts)


def owner_gates(incoming, router_full):
    logits = jnp.einsum("sjcd,de->sjce", incoming, router_full, preferred_element_type=jnp.float32)
    router_probs, _ = softmax_rows(logits)
    local = incoming.shape[1]
    own = lax.axis_index("expert") * local + jnp.arange(local, dtype=jnp.int32)
    labels = jnp.arange(router_full.shape[1], dtype=jnp.int32)
    pick = (own[:, None] == labels[None, :]).astype(jnp.float32)
    return jnp.sum(router_probs * pick[None, :, None, :], axis=-1, keepdims=True)


def gather_experts(which, w_first, w_second):
    first_full = lax.all_gather(w_first[which], "dp", axis=2, tiled=True)
    second_full = lax.all_gather(w_second[which], "dp", axis=1, tiled=True)
    return (first_full, second_full)


def route_tables(route, experts_total, capacity):
    labels = jnp.arange(experts_total, dtype=jnp.int32)
    pick_first = (route[:, 0:1] == labels[None, :]).astype(jnp.int32)
    pick_second = (route[:, 1:2] == labels[None, :]).astype(jnp.int32)
    both_picks = pick_first + pick_second
    before = jnp.cumsum(both_picks, axis=0) - both_picks
    slot_first = route[:, 0] * capacity + jnp.sum(before * pick_first, axis=1)
    slot_second = route[:, 1] * capacity + jnp.sum(before * pick_second, axis=1)
    slot_ids = jnp.arange(experts_total * capacity, dtype=jnp.int32)
    place_first = (slot_ids[:, None] == slot_first[None, :]).astype(jnp.bfloat16)
    place_second = (slot_ids[:, None] == slot_second[None, :]).astype(jnp.bfloat16)
    return (
        pick_first.astype(jnp.float32),
        pick_second.astype(jnp.float32),
        place_first,
        place_second,
    )


def exchange(block):
    return lax.all_to_all(block, "expert", split_axis=0, concat_axis=0, tiled=True)


def attend_forward(resid, dense, tables):
    qkv_full, proj_full, router_full, gains_wide, shifts_wide = dense
    pick_first_f, pick_second_f, _, _ = tables
    tok_count, width = resid.shape
    images = tok_count // SEQ
    attn_norm, unit_a, inv_a = layer_norm(resid, gains_wide[0], shifts_wide[0])
    attn_in = attn_norm.astype(jnp.bfloat16)
    packed = jnp.dot(attn_in, qkv_full, preferred_element_type=jnp.float32)
    head_shape = (images, SEQ, HEADS, HEAD_DIM)
    query = (packed[:, :width] * HEAD_DIM ** (-0.5)).astype(jnp.bfloat16).reshape(head_shape)
    keyed = packed[:, width : 2 * width].astype(jnp.bfloat16).reshape(head_shape)
    valued = packed[:, 2 * width :].astype(jnp.bfloat16).reshape(head_shape)
    scores = jnp.einsum("iqhd,ikhd->ihqk", query, keyed, preferred_element_type=jnp.float32)
    probs, log_total = softmax_rows(scores)
    mixed = jnp.einsum(
        "ihqk,ikhd->iqhd", probs.astype(jnp.bfloat16), valued, preferred_element_type=jnp.float32
    )
    mixed = mixed.reshape(tok_count, width).astype(jnp.bfloat16)
    resid_mid = resid + jnp.dot(mixed, proj_full, preferred_element_type=jnp.float32)
    moe_norm, unit_b, inv_b = layer_norm(resid_mid, gains_wide[1], shifts_wide[1])
    moe_in = moe_norm.astype(jnp.bfloat16)
    logits = jnp.dot(moe_in, router_full, preferred_element_type=jnp.float32)
    router_probs, _ = softmax_rows(logits)
    gate_first = jnp.sum(router_probs * pick_first_f, axis=1)
    gate_second = jnp.sum(router_probs * pick_second_f, axis=1)
    router_probs, gate_first, gate_second = lax.optimization_barrier(
        (router_probs, gate_first, gate_second)
    )
    attn_saved = (unit_a, inv_a, attn_in, query, keyed, valued, log_total, mixed)
    moe_saved = (unit_b, inv_b, moe_in, router_probs, gate_first, gate_second)
    return (resid_mid, attn_saved, moe_saved)


def slots_of(rows, place, block_shape):
    slots = jnp.dot(place, rows, preferred_element_type=jnp.float32)
    return slots.astype(jnp.bfloat16).reshape(block_shape)


def gated_slots(grad_out, moe_saved, tables, block_shape):
    gate_first, gate_second = moe_saved[4:]
    place_first, place_second = tables[2:]
    send_first = (gate_first[:, None] * grad_out).astype(jnp.bfloat16)
    send_second = (gate_second[:, None] * grad_out).astype(jnp.bfloat16)
    slots = jnp.dot(place_first, send_first, preferred_element_type=jnp.float32) + jnp.dot(
        place_second, send_second, preferred_element_type=jnp.float32
    )
    return slots.astype(jnp.bfloat16).reshape(block_shape)


def experts_hidden(incoming, first_full):
    hidden_pre = jnp.einsum(
        "sjcd,jdf->sjcf", incoming, first_full, preferred_element_type=jnp.float32
    )
    return (hidden_pre, gelu_value(hidden_pre).astype(jnp.bfloat16))


def experts_result(hidden_act, second_full):
    return jnp.einsum(
        "sjcf,jfd->sjcd", hidden_act, second_full, preferred_element_type=jnp.float32
    ).astype(jnp.bfloat16)


def rows_back(returned, place):
    return jnp.einsum("st,sd->td", place, returned, preferred_element_type=jnp.float32)


def experts_backward(grad_result, incoming, hidden_pre, hidden_act, experts):
    first_full, second_full = experts
    grad_second = jnp.einsum(
        "sjcf,sjcd->jfd", hidden_act, grad_result, preferred_element_type=jnp.float32
    ).astype(jnp.bfloat16)
    share_second = lax.psum_scatter(grad_second, "dp", scatter_dimension=1, tiled=True)
    grad_act = jnp.einsum(
        "sjcd,jfd->sjcf", grad_result, second_full, preferred_element_type=jnp.float32
    )
    grad_pre = (grad_act * gelu_slope(hidden_pre)).astype(jnp.bfloat16)
    grad_rows = jnp.einsum(
        "sjcf,jdf->sjcd", grad_pre, first_full, preferred_element_type=jnp.float32
    ).astype(jnp.bfloat16)
    grad_back = exchange(grad_rows)
    grad_first = jnp.einsum(
        "sjcd,sjcf->jdf", incoming, grad_pre, preferred_element_type=jnp.float32
    ).astype(jnp.bfloat16)
    grad_back, grad_first = lax.optimization_barrier((grad_back, grad_first))
    share_first = lax.psum_scatter(grad_first, "dp", scatter_dimension=2, tiled=True)
    return (grad_back, share_first, share_second)


def tokens_backward(grad_out, grad_back, backs, dense, tables, attn_saved, moe_saved):
    qkv_full, proj_full, router_full, gains_wide, _ = dense
    pick_first_f, pick_second_f, place_first, place_second = tables
    unit_a, inv_a, attn_in, query, keyed, valued, log_total, mixed = attn_saved
    unit_b, inv_b, moe_in, router_probs, _, _ = moe_saved
    tok_count, width = grad_out.shape
    images = tok_count // SEQ
    grad_gate_first = jnp.sum(grad_out * backs[0], axis=1)
    grad_gate_second = jnp.sum(grad_out * backs[1], axis=1)
    grad_back = grad_back.reshape(-1, width)
    grad_moe = rows_back(grad_back, place_first + place_second)
    grad_probs = pick_first_f * grad_gate_first[:, None] + pick_second_f * grad_gate_second[:, None]
    weighted = jnp.sum(router_probs * grad_probs, axis=1, keepdims=True)
    grad_logits = (router_probs * (grad_probs - weighted)).astype(jnp.bfloat16)
    grad_router = jnp.einsum("td,te->de", moe_in, grad_logits, preferred_element_type=jnp.float32)
    grad_moe = grad_moe + jnp.einsum(
        "te,de->td", grad_logits, router_full, preferred_element_type=jnp.float32
    )
    grad_norm_b, gain_b_grad, shift_b_grad = norm_back(grad_moe, unit_b, inv_b, gains_wide[1])
    grad_mid = grad_out + grad_norm_b
    grad_branch = grad_mid.astype(jnp.bfloat16)
    grad_proj = jnp.einsum("td,te->de", mixed, grad_branch, preferred_element_type=jnp.float32)
    grad_mixed = jnp.einsum("te,de->td", grad_branch, proj_full, preferred_element_type=jnp.float32)
    grad_mixed = grad_mixed.astype(jnp.bfloat16).reshape(images, SEQ, HEADS, HEAD_DIM)
    scores = jnp.einsum("iqhd,ikhd->ihqk", query, keyed, preferred_element_type=jnp.float32)
    probs = jnp.exp(scores - log_total)
    grad_weights = jnp.einsum(
        "iqhd,ikhd->ihqk", grad_mixed, valued, preferred_element_type=jnp.float32
    )
    grad_valued = jnp.einsum(
        "ihqk,iqhd->ikhd",
        probs.astype(jnp.bfloat16),
        grad_mixed,
        preferred_element_type=jnp.float32,
    ).astype(jnp.bfloat16)
    row_inner = jnp.sum(probs * grad_weights, axis=-1, keepdims=True)
    grad_scores = (probs * (grad_weights - row_inner)).astype(jnp.bfloat16)
    grad_query = jnp.einsum(
        "ihqk,ikhd->iqhd", grad_scores, keyed, preferred_element_type=jnp.float32
    ).astype(jnp.bfloat16)
    grad_query = grad_query * jnp.asarray(HEAD_DIM ** (-0.5), jnp.bfloat16)
    grad_keyed = jnp.einsum(
        "ihqk,iqhd->ikhd", grad_scores, query, preferred_element_type=jnp.float32
    ).astype(jnp.bfloat16)
    grad_packed = jnp.concatenate(
        [
            grad_query.reshape(tok_count, width),
            grad_keyed.reshape(tok_count, width),
            grad_valued.reshape(tok_count, width),
        ],
        axis=1,
    )
    grad_qkv = jnp.einsum("td,te->de", attn_in, grad_packed, preferred_element_type=jnp.float32)
    grad_attn = jnp.einsum("te,de->td", grad_packed, qkv_full, preferred_element_type=jnp.float32)
    grad_norm_a, gain_a_grad, shift_a_grad = norm_back(grad_attn, unit_a, inv_a, gains_wide[0])
    grad_in = grad_mid + grad_norm_a
    low = jnp.bfloat16
    small = jnp.concatenate(
        [
            grad_qkv.astype(low),
            grad_proj.astype(low),
            grad_router.astype(low),
            jnp.stack([gain_a_grad, gain_b_grad, shift_a_grad, shift_b_grad], axis=1).astype(low),
        ],
        axis=1,
    )
    peers, shares = lax.axis_size("expert"), lax.axis_size("dp")
    piece = width // (peers * shares)
    columns = small.shape[1]
    small = small.reshape(shares, peers, piece, columns).swapaxes(0, 1)
    small = exchange(small)
    small = jnp.sum(small.astype(jnp.float32), axis=0).astype(low)
    return (grad_in, small)


def whole_step(
    embedded, cotangent, w_qkv, w_proj, w_router, norm_gains, norm_shifts, w_first, w_second, routes
):
    images, length, width = embedded.shape
    tok_count = images * length
    experts_total = w_router.shape[2]
    peers = lax.axis_size("expert")
    capacity = -(-max(2, 3 * tok_count // experts_total) // 8) * 8
    block_shape = (peers, experts_total // peers, capacity, width)
    resid = embedded.reshape(tok_count, width).astype(jnp.float32)
    grad = cotangent.reshape(tok_count, width).astype(jnp.float32)
    dense, experts, tables = [], [], []
    quarters = gather_quarters(w_qkv, w_proj, w_router, norm_gains, norm_shifts)
    for which in range(LAYERS):
        experts.append(gather_experts(which, w_first, w_second))
        tables.append(
            route_tables(routes[which].reshape(tok_count, 2), experts_total, capacity)
        )
    last = tables[LAYERS - 1]
    slots = slots_of(cotangent.reshape(tok_count, width), last[2] + last[3], block_shape)
    cot_rows = exchange(slots)
    for which in range(LAYERS):
        dense.append(spread_dense(quarters[which], experts_total))
    attn_saved, moe_saved, kept = [], [], []
    grad_result = None
    for which in range(LAYERS):
        table = tables[which]
        resid_mid, attn_part, moe_part = attend_forward(resid, dense[which], table)
        outgoing = slots_of(moe_part[2], table[2] + table[3], block_shape)
        incoming = exchange(outgoing)
        hidden_pre, hidden_act = experts_hidden(incoming, experts[which][0])
        if which == LAYERS - 1:
            gates = owner_gates(incoming, dense[which][2])
            grad_result = (gates * cot_rows.astype(jnp.float32)).astype(jnp.bfloat16)
        result = experts_result(hidden_act, experts[which][1])
        returned = exchange(result).reshape(experts_total * capacity, width)
        backs = (rows_back(returned, table[2]), rows_back(returned, table[3]))
        resid = resid_mid + (
            moe_part[4][:, None] * backs[0] + moe_part[5][:, None] * backs[1]
        )
        attn_saved.append(attn_part)
        moe_saved.append(moe_part)
        kept.append((incoming, hidden_pre, hidden_act, backs))
    out_images = resid.reshape(images, length, width).astype(jnp.bfloat16)
    smalls, firsts, seconds = [None] * LAYERS, [None] * LAYERS, [None] * LAYERS
    for which in reversed(range(LAYERS)):
        incoming, hidden_pre, hidden_act, backs = kept[which]
        if which < LAYERS - 1:
            slots = gated_slots(grad, moe_saved[which], tables[which], block_shape)
            grad_result = exchange(slots)
        grad_back, firsts[which], seconds[which] = experts_backward(
            grad_result, incoming, hidden_pre, hidden_act, experts[which]
        )
        grad, smalls[which] = tokens_backward(
            grad,
            grad_back,
            backs,
            dense[which],
            tables[which],
            attn_saved[which],
            moe_saved[which],
        )
    both = jnp.stack(smalls, axis=2)
    both = lax.psum_scatter(both, "dp", scatter_dimension=0, tiled=True)[0]
    total = lax.all_gather(both, "expert", axis=0, tiled=True)
    total = total.swapaxes(0, 1).astype(jnp.float32)
    grad_images = grad.reshape(images, length, width)
    wide = total[:, :, 4 * width :]
    return (
        out_images,
        grad_images,
        total[:, :, : 3 * width],
        total[:, :, 3 * width : 4 * width],
        wide[:, :, :experts_total],
        jnp.swapaxes(wide[:, :, experts_total : experts_total + 2], 1, 2),
        jnp.swapaxes(wide[:, :, experts_total + 2 :], 1, 2),
        jnp.stack(firsts).astype(jnp.float32),
        jnp.stack(seconds).astype(jnp.float32),
    )


def solution(mesh):

    return jax.shard_map(
        whole_step,
        mesh=mesh,
        in_specs=(
            P(("dp", "expert"), None, None),
            P(("dp", "expert"), None, None),
            P(None, "dp", None),
            P(None, "dp", None),
            P(None, "dp", None),
            P(None, None, "dp"),
            P(None, None, "dp"),
            P(None, "expert", None, "dp"),
            P(None, "expert", "dp", None),
            P(None, ("dp", "expert"), None, None),
        ),
        out_specs=(
            P(("dp", "expert"), None, None),
            P(("dp", "expert"), None, None),
            P(None, "dp", None),
            P(None, "dp", None),
            P(None, "dp", None),
            P(None, None, "dp"),
            P(None, None, "dp"),
            P(None, "expert", None, "dp"),
            P(None, "expert", "dp", None),
        ),
        check_vma=False,
    )
```

```python
import jax
import jax.numpy as jnp
from jax import lax
from jax.experimental import pallas as pl
from jax.sharding import PartitionSpec as P

HEADS = 8
HEAD_DIM = 64
SEQ = 197
SEQ_PAD = 208
LAYERS = 2
ROW_DOTS = (((1,), (1,)), ((), ()))
COL_DOTS = (((0,), (0,)), ((), ()))


EPSILON = 1e-06
ROOT_HALF = 0.7071067811865476
INV_ROOT_TAU = 0.3989422804014327


def layer_norm(values, scale_in, shift_in):
    center = values - jnp.mean(values, axis=-1, keepdims=True)
    variance = jnp.mean(center * center, axis=-1, keepdims=True)
    inverse = lax.rsqrt(variance + EPSILON)
    normed = center * inverse
    return (normed * scale_in + shift_in, normed, inverse)


def norm_back(grad_out, normed, inverse, scale_in):
    grad_normed = grad_out * scale_in
    first_mean = jnp.mean(grad_normed, axis=-1, keepdims=True)
    second_mean = jnp.mean(grad_normed * normed, axis=-1, keepdims=True)
    grad_in = inverse * (grad_normed - first_mean - normed * second_mean)
    return (grad_in, jnp.sum(grad_out * normed, axis=0), jnp.sum(grad_out, axis=0))


def softmax_rows(scores):
    highest = jnp.max(scores, axis=-1, keepdims=True)
    powers = jnp.exp(scores - highest)
    row_total = jnp.sum(powers, axis=-1, keepdims=True)
    return (powers / row_total, highest + jnp.log(row_total))


def gelu_value(preact):
    return 0.5 * preact * (1.0 + lax.erf(preact * ROOT_HALF))


def gelu_slope(preact):
    return (
        0.5 * (1.0 + lax.erf(preact * ROOT_HALF))
        + preact * jnp.exp(-0.5 * preact * preact) * INV_ROOT_TAU
    )


def gather_quarters(w_qkv, w_proj, w_router, norm_gains, norm_shifts):
    peers, rank = lax.axis_size("expert"), lax.axis_index("expert")
    piece = w_qkv.shape[1] // peers
    packed = jnp.concatenate(
        [w_qkv, w_proj, w_router, jnp.swapaxes(norm_gains, 1, 2), jnp.swapaxes(norm_shifts, 1, 2)],
        axis=2,
    )
    packed = lax.dynamic_slice_in_dim(packed, rank * piece, piece, axis=1)
    return lax.all_gather(packed, "dp", axis=1, tiled=True)


def spread_dense(quarter, experts):
    peers, shares = lax.axis_size("expert"), lax.axis_size("dp")
    rows, columns = quarter.shape
    parts = exchange(jnp.broadcast_to(quarter[None], (peers, rows, columns)))
    width = peers * rows
    parts = parts.reshape(peers, shares, rows // shares, columns)

    def whole(start, stop):
        return parts[..., start:stop].swapaxes(0, 1).reshape(width, stop - start)

    base = 4 * width
    wide = whole(base, columns)
    gains = wide[:, experts : experts + 2].T.astype(jnp.float32)
    shifts = wide[:, experts + 2 : experts + 4].T.astype(jnp.float32)
    return (whole(0, 3 * width), whole(3 * width, base), wide[:, :experts], gains, shifts)


def owner_gates(incoming, router_full):
    logits = jnp.einsum("sjcd,de->sjce", incoming, router_full, preferred_element_type=jnp.float32)
    router_probs, _ = softmax_rows(logits)
    local = incoming.shape[1]
    own = lax.axis_index("expert") * local + jnp.arange(local, dtype=jnp.int32)
    labels = jnp.arange(router_full.shape[1], dtype=jnp.int32)
    pick = (own[:, None] == labels[None, :]).astype(jnp.float32)
    return jnp.sum(router_probs * pick[None, :, None, :], axis=-1, keepdims=True)


def gather_experts(which, w_first, w_second):
    first_full = lax.all_gather(w_first[which], "dp", axis=2, tiled=True)
    second_full = lax.all_gather(w_second[which], "dp", axis=1, tiled=True)
    return (first_full, second_full)


def route_tables(route, experts_total, capacity):
    labels = jnp.arange(experts_total, dtype=jnp.int32)
    pick_first = (route[:, 0:1] == labels[None, :]).astype(jnp.int32)
    pick_second = (route[:, 1:2] == labels[None, :]).astype(jnp.int32)
    both_picks = pick_first + pick_second
    before = jnp.cumsum(both_picks, axis=0) - both_picks
    slot_first = route[:, 0] * capacity + jnp.sum(before * pick_first, axis=1)
    slot_second = route[:, 1] * capacity + jnp.sum(before * pick_second, axis=1)
    slot_ids = jnp.arange(experts_total * capacity, dtype=jnp.int32)
    place_first = (slot_ids[:, None] == slot_first[None, :]).astype(jnp.bfloat16)
    place_second = (slot_ids[:, None] == slot_second[None, :]).astype(jnp.bfloat16)
    return (
        pick_first.astype(jnp.float32),
        pick_second.astype(jnp.float32),
        place_first,
        place_second,
    )


def exchange(block):
    return lax.all_to_all(block, "expert", split_axis=0, concat_axis=0, tiled=True)


def head_of(ref, part, head):
    start = part * HEADS * HEAD_DIM + head * HEAD_DIM
    return ref[:, start : start + HEAD_DIM]


def masked_scores(query, keyed):
    scores = lax.dot_general(query, keyed, ROW_DOTS, preferred_element_type=jnp.float32)
    columns = lax.broadcasted_iota(jnp.int32, scores.shape, 1)
    return jnp.where(columns < SEQ, scores, -1e30)


def attention_kernel(packed_ref, mixed_ref, total_ref):
    scale = jnp.asarray(HEAD_DIM ** (-0.5), jnp.bfloat16)
    mixed, totals = [], []
    for head in range(HEADS):
        query = head_of(packed_ref, 0, head) * scale
        scores = masked_scores(query, head_of(packed_ref, 1, head))
        highest = jnp.max(scores, axis=-1, keepdims=True)
        powers = jnp.exp(scores - highest)
        row_total = jnp.sum(powers, axis=-1, keepdims=True)
        probs = (powers * (1.0 / row_total)).astype(jnp.bfloat16)
        mixed.append(
            jnp.dot(
                probs, head_of(packed_ref, 2, head), preferred_element_type=jnp.float32
            ).astype(jnp.bfloat16)
        )
        totals.append(highest + jnp.log(row_total))
    mixed_ref[...] = jnp.concatenate(mixed, axis=1)
    total_ref[...] = jnp.concatenate(totals, axis=1)


def attention_back_kernel(packed_ref, grad_ref, total_ref, out_ref):
    scale = jnp.asarray(HEAD_DIM ** (-0.5), jnp.bfloat16)
    queries, keys, values = [], [], []
    for head in range(HEADS):
        query = head_of(packed_ref, 0, head) * scale
        keyed = head_of(packed_ref, 1, head)
        grad_mixed = head_of(grad_ref, 0, head)
        scores = masked_scores(query, keyed)
        probs = jnp.exp(scores - total_ref[:, head : head + 1])
        grad_probs = lax.dot_general(
            grad_mixed,
            head_of(packed_ref, 2, head),
            ROW_DOTS,
            preferred_element_type=jnp.float32,
        )
        values.append(
            lax.dot_general(
                probs.astype(jnp.bfloat16),
                grad_mixed,
                COL_DOTS,
                preferred_element_type=jnp.float32,
            ).astype(jnp.bfloat16)
        )
        row_inner = jnp.sum(probs * grad_probs, axis=-1, keepdims=True)
        grad_scores = (probs * (grad_probs - row_inner)).astype(jnp.bfloat16)
        grad_query = jnp.dot(grad_scores, keyed, preferred_element_type=jnp.float32)
        queries.append(grad_query.astype(jnp.bfloat16) * scale)
        keys.append(
            lax.dot_general(
                grad_scores, query, COL_DOTS, preferred_element_type=jnp.float32
            ).astype(jnp.bfloat16)
        )
    out_ref[...] = jnp.concatenate(queries + keys + values, axis=1)


def image_block(columns):
    return pl.BlockSpec((SEQ_PAD, columns), lambda image: (image, 0))


def attention(packed):
    rows, columns = packed.shape
    width = columns // 3
    return pl.pallas_call(
        attention_kernel,
        grid=(rows // SEQ_PAD,),
        in_specs=[image_block(columns)],
        out_specs=[image_block(width), image_block(HEADS)],
        out_shape=[
            jax.ShapeDtypeStruct((rows, width), jnp.bfloat16),
            jax.ShapeDtypeStruct((rows, HEADS), jnp.float32),
        ],
        name="attention",
    )(packed)


def attention_back(packed, grad_mixed, totals):
    rows, columns = packed.shape
    return pl.pallas_call(
        attention_back_kernel,
        grid=(rows // SEQ_PAD,),
        in_specs=[image_block(columns), image_block(columns // 3), image_block(HEADS)],
        out_specs=image_block(columns),
        out_shape=jax.ShapeDtypeStruct((rows, columns), jnp.bfloat16),
        name="attention_back",
    )(packed, grad_mixed, totals)


def attend_forward(resid, dense, tables):
    qkv_full, proj_full, router_full, gains_wide, shifts_wide = dense
    pick_first_f, pick_second_f, _, _ = tables
    attn_norm, unit_a, inv_a = layer_norm(resid, gains_wide[0], shifts_wide[0])
    attn_in = attn_norm.astype(jnp.bfloat16)
    packed = jnp.dot(attn_in, qkv_full, preferred_element_type=jnp.float32)
    packed = packed.astype(jnp.bfloat16)
    mixed, totals = attention(packed)
    resid_mid = resid + jnp.dot(mixed, proj_full, preferred_element_type=jnp.float32)
    moe_norm, unit_b, inv_b = layer_norm(resid_mid, gains_wide[1], shifts_wide[1])
    moe_in = moe_norm.astype(jnp.bfloat16)
    logits = jnp.dot(moe_in, router_full, preferred_element_type=jnp.float32)
    router_probs, _ = softmax_rows(logits)
    gate_first = jnp.sum(router_probs * pick_first_f, axis=1)
    gate_second = jnp.sum(router_probs * pick_second_f, axis=1)
    router_probs, gate_first, gate_second = lax.optimization_barrier(
        (router_probs, gate_first, gate_second)
    )
    attn_saved = (unit_a, inv_a, attn_in, packed, totals, mixed)
    moe_saved = (unit_b, inv_b, moe_in, router_probs, gate_first, gate_second)
    return (resid_mid, attn_saved, moe_saved)


def slots_of(rows, place, block_shape):
    slots = jnp.dot(place, rows, preferred_element_type=jnp.float32)
    return slots.astype(jnp.bfloat16).reshape(block_shape)


def gated_slots(grad_out, moe_saved, tables, block_shape):
    gate_first, gate_second = moe_saved[4:]
    place_first, place_second = tables[2:]
    send_first = (gate_first[:, None] * grad_out).astype(jnp.bfloat16)
    send_second = (gate_second[:, None] * grad_out).astype(jnp.bfloat16)
    slots = jnp.dot(place_first, send_first, preferred_element_type=jnp.float32) + jnp.dot(
        place_second, send_second, preferred_element_type=jnp.float32
    )
    return slots.astype(jnp.bfloat16).reshape(block_shape)


def experts_hidden(incoming, first_full):
    hidden_pre = jnp.einsum(
        "sjcd,jdf->sjcf", incoming, first_full, preferred_element_type=jnp.float32
    )
    return (hidden_pre, gelu_value(hidden_pre).astype(jnp.bfloat16))


def experts_result(hidden_act, second_full):
    return jnp.einsum(
        "sjcf,jfd->sjcd", hidden_act, second_full, preferred_element_type=jnp.float32
    ).astype(jnp.bfloat16)


def rows_back(returned, place):
    return jnp.einsum("st,sd->td", place, returned, preferred_element_type=jnp.float32)


def experts_backward(grad_result, incoming, hidden_pre, hidden_act, experts):
    first_full, second_full = experts
    grad_second = jnp.einsum(
        "sjcf,sjcd->jfd", hidden_act, grad_result, preferred_element_type=jnp.float32
    ).astype(jnp.bfloat16)
    share_second = lax.psum_scatter(grad_second, "dp", scatter_dimension=1, tiled=True)
    grad_act = jnp.einsum(
        "sjcd,jfd->sjcf", grad_result, second_full, preferred_element_type=jnp.float32
    )
    grad_pre = (grad_act * gelu_slope(hidden_pre)).astype(jnp.bfloat16)
    grad_rows = jnp.einsum(
        "sjcf,jdf->sjcd", grad_pre, first_full, preferred_element_type=jnp.float32
    ).astype(jnp.bfloat16)
    grad_back = exchange(grad_rows)
    grad_first = jnp.einsum(
        "sjcd,sjcf->jdf", incoming, grad_pre, preferred_element_type=jnp.float32
    ).astype(jnp.bfloat16)
    grad_back, grad_first = lax.optimization_barrier((grad_back, grad_first))
    share_first = lax.psum_scatter(grad_first, "dp", scatter_dimension=2, tiled=True)
    return (grad_back, share_first, share_second)


def tokens_backward(grad_out, grad_back, backs, dense, tables, attn_saved, moe_saved):
    qkv_full, proj_full, router_full, gains_wide, _ = dense
    pick_first_f, pick_second_f, place_first, place_second = tables
    unit_a, inv_a, attn_in, packed, totals, mixed = attn_saved
    unit_b, inv_b, moe_in, router_probs, _, _ = moe_saved
    width = grad_out.shape[1]
    grad_gate_first = jnp.sum(grad_out * backs[0], axis=1)
    grad_gate_second = jnp.sum(grad_out * backs[1], axis=1)
    grad_back = grad_back.reshape(-1, width)
    grad_moe = rows_back(grad_back, place_first + place_second)
    grad_probs = pick_first_f * grad_gate_first[:, None] + pick_second_f * grad_gate_second[:, None]
    weighted = jnp.sum(router_probs * grad_probs, axis=1, keepdims=True)
    grad_logits = (router_probs * (grad_probs - weighted)).astype(jnp.bfloat16)
    grad_router = jnp.einsum("td,te->de", moe_in, grad_logits, preferred_element_type=jnp.float32)
    grad_moe = grad_moe + jnp.einsum(
        "te,de->td", grad_logits, router_full, preferred_element_type=jnp.float32
    )
    grad_norm_b, gain_b_grad, shift_b_grad = norm_back(grad_moe, unit_b, inv_b, gains_wide[1])
    grad_mid = grad_out + grad_norm_b
    grad_branch = grad_mid.astype(jnp.bfloat16)
    grad_proj = jnp.einsum("td,te->de", mixed, grad_branch, preferred_element_type=jnp.float32)
    grad_mixed = jnp.einsum("te,de->td", grad_branch, proj_full, preferred_element_type=jnp.float32)
    grad_packed = attention_back(packed, grad_mixed.astype(jnp.bfloat16), totals)
    grad_qkv = jnp.einsum("td,te->de", attn_in, grad_packed, preferred_element_type=jnp.float32)
    grad_attn = jnp.einsum("te,de->td", grad_packed, qkv_full, preferred_element_type=jnp.float32)
    grad_norm_a, gain_a_grad, shift_a_grad = norm_back(grad_attn, unit_a, inv_a, gains_wide[0])
    grad_in = grad_mid + grad_norm_a
    low = jnp.bfloat16
    small = jnp.concatenate(
        [
            grad_qkv.astype(low),
            grad_proj.astype(low),
            grad_router.astype(low),
            jnp.stack([gain_a_grad, gain_b_grad, shift_a_grad, shift_b_grad], axis=1).astype(low),
        ],
        axis=1,
    )
    peers, shares = lax.axis_size("expert"), lax.axis_size("dp")
    piece = width // (peers * shares)
    columns = small.shape[1]
    small = small.reshape(shares, peers, piece, columns).swapaxes(0, 1)
    small = exchange(small)
    small = jnp.sum(small.astype(jnp.float32), axis=0).astype(low)
    return (grad_in, small)


def whole_step(
    embedded, cotangent, w_qkv, w_proj, w_router, norm_gains, norm_shifts, w_first, w_second, routes
):
    images, length, width = embedded.shape
    tok_count = images * length
    experts_total = w_router.shape[2]
    peers = lax.axis_size("expert")
    capacity = -(-max(2, 3 * tok_count // experts_total) // 8) * 8
    block_shape = (peers, experts_total // peers, capacity, width)
    fill = ((0, 0), (0, SEQ_PAD - length), (0, 0))
    rows = images * SEQ_PAD
    cot_low = jnp.pad(cotangent, fill).reshape(rows, width)
    resid = jnp.pad(embedded, fill).reshape(rows, width).astype(jnp.float32)
    grad = cot_low.astype(jnp.float32)
    dense, experts, tables = [], [], []
    quarters = gather_quarters(w_qkv, w_proj, w_router, norm_gains, norm_shifts)
    for which in range(LAYERS):
        experts.append(gather_experts(which, w_first, w_second))
        route = jnp.pad(routes[which], fill, constant_values=experts_total).reshape(rows, 2)
        tables.append(route_tables(route, experts_total, capacity))
    last = tables[LAYERS - 1]
    slots = slots_of(cot_low, last[2] + last[3], block_shape)
    cot_rows = exchange(slots)
    for which in range(LAYERS):
        dense.append(spread_dense(quarters[which], experts_total))
    attn_saved, moe_saved, kept = [], [], []
    grad_result = None
    for which in range(LAYERS):
        table = tables[which]
        resid_mid, attn_part, moe_part = attend_forward(resid, dense[which], table)
        outgoing = slots_of(moe_part[2], table[2] + table[3], block_shape)
        incoming = exchange(outgoing)
        hidden_pre, hidden_act = experts_hidden(incoming, experts[which][0])
        if which == LAYERS - 1:
            gates = owner_gates(incoming, dense[which][2])
            grad_result = (gates * cot_rows.astype(jnp.float32)).astype(jnp.bfloat16)
        result = experts_result(hidden_act, experts[which][1])
        returned = exchange(result).reshape(experts_total * capacity, width)
        backs = (rows_back(returned, table[2]), rows_back(returned, table[3]))
        resid = resid_mid + (
            moe_part[4][:, None] * backs[0] + moe_part[5][:, None] * backs[1]
        )
        attn_saved.append(attn_part)
        moe_saved.append(moe_part)
        kept.append((incoming, hidden_pre, hidden_act, backs))
    out_images = resid.reshape(images, SEQ_PAD, width)[:, :length].astype(jnp.bfloat16)
    smalls, firsts, seconds = [None] * LAYERS, [None] * LAYERS, [None] * LAYERS
    for which in reversed(range(LAYERS)):
        incoming, hidden_pre, hidden_act, backs = kept[which]
        if which < LAYERS - 1:
            slots = gated_slots(grad, moe_saved[which], tables[which], block_shape)
            grad_result = exchange(slots)
        grad_back, firsts[which], seconds[which] = experts_backward(
            grad_result, incoming, hidden_pre, hidden_act, experts[which]
        )
        grad, smalls[which] = tokens_backward(
            grad,
            grad_back,
            backs,
            dense[which],
            tables[which],
            attn_saved[which],
            moe_saved[which],
        )
    both = jnp.stack(smalls, axis=2)
    both = lax.psum_scatter(both, "dp", scatter_dimension=0, tiled=True)[0]
    total = lax.all_gather(both, "expert", axis=0, tiled=True)
    total = total.swapaxes(0, 1).astype(jnp.float32)
    grad_images = grad.reshape(images, SEQ_PAD, width)[:, :length]
    wide = total[:, :, 4 * width :]
    return (
        out_images,
        grad_images,
        total[:, :, : 3 * width],
        total[:, :, 3 * width : 4 * width],
        wide[:, :, :experts_total],
        jnp.swapaxes(wide[:, :, experts_total : experts_total + 2], 1, 2),
        jnp.swapaxes(wide[:, :, experts_total + 2 :], 1, 2),
        jnp.stack(firsts).astype(jnp.float32),
        jnp.stack(seconds).astype(jnp.float32),
    )


def solution(mesh):

    return jax.shard_map(
        whole_step,
        mesh=mesh,
        in_specs=(
            P(("dp", "expert"), None, None),
            P(("dp", "expert"), None, None),
            P(None, "dp", None),
            P(None, "dp", None),
            P(None, "dp", None),
            P(None, None, "dp"),
            P(None, None, "dp"),
            P(None, "expert", None, "dp"),
            P(None, "expert", "dp", None),
            P(None, ("dp", "expert"), None, None),
        ),
        out_specs=(
            P(("dp", "expert"), None, None),
            P(("dp", "expert"), None, None),
            P(None, "dp", None),
            P(None, "dp", None),
            P(None, "dp", None),
            P(None, None, "dp"),
            P(None, None, "dp"),
            P(None, "expert", None, "dp"),
            P(None, "expert", "dp", None),
        ),
        check_vma=False,
    )
```

```python
import jax
import jax.numpy as jnp
from jax import lax
from jax.experimental import pallas as pl
from jax.sharding import PartitionSpec as P

HEADS = 8
HEAD_DIM = 64
SEQ = 197
SEQ_PAD = 208
LAYERS = 2
ROW_DOTS = (((1,), (1,)), ((), ()))
COL_DOTS = (((0,), (0,)), ((), ()))


EPSILON = 1e-06
ROOT_HALF = 0.7071067811865476
INV_ROOT_TAU = 0.3989422804014327


def layer_norm(values, scale_in, shift_in):
    center = values - jnp.mean(values, axis=-1, keepdims=True)
    variance = jnp.mean(center * center, axis=-1, keepdims=True)
    inverse = lax.rsqrt(variance + EPSILON)
    normed = center * inverse
    return (normed * scale_in + shift_in, normed, inverse)


def norm_back(grad_out, normed, inverse, scale_in):
    grad_normed = grad_out * scale_in
    first_mean = jnp.mean(grad_normed, axis=-1, keepdims=True)
    second_mean = jnp.mean(grad_normed * normed, axis=-1, keepdims=True)
    grad_in = inverse * (grad_normed - first_mean - normed * second_mean)
    return (grad_in, jnp.sum(grad_out * normed, axis=0), jnp.sum(grad_out, axis=0))


def softmax_rows(scores):
    highest = jnp.max(scores, axis=-1, keepdims=True)
    powers = jnp.exp(scores - highest)
    row_total = jnp.sum(powers, axis=-1, keepdims=True)
    return (powers / row_total, highest + jnp.log(row_total))


def gelu_value(preact):
    return 0.5 * preact * (1.0 + lax.erf(preact * ROOT_HALF))


def gelu_slope(preact):
    return (
        0.5 * (1.0 + lax.erf(preact * ROOT_HALF))
        + preact * jnp.exp(-0.5 * preact * preact) * INV_ROOT_TAU
    )


def gather_quarters(w_qkv, w_proj, w_router, norm_gains, norm_shifts):
    peers, rank = lax.axis_size("expert"), lax.axis_index("expert")
    piece = w_qkv.shape[1] // peers
    packed = jnp.concatenate(
        [w_qkv, w_proj, w_router, jnp.swapaxes(norm_gains, 1, 2), jnp.swapaxes(norm_shifts, 1, 2)],
        axis=2,
    )
    packed = lax.dynamic_slice_in_dim(packed, rank * piece, piece, axis=1)
    return lax.all_gather(packed, "dp", axis=1, tiled=True)


def spread_dense(quarter, experts):
    peers, shares = lax.axis_size("expert"), lax.axis_size("dp")
    rows, columns = quarter.shape
    parts = exchange(jnp.broadcast_to(quarter[None], (peers, rows, columns)))
    width = peers * rows
    parts = parts.reshape(peers, shares, rows // shares, columns)

    def whole(start, stop):
        return parts[..., start:stop].swapaxes(0, 1).reshape(width, stop - start)

    base = 4 * width
    wide = whole(base, columns)
    gains = wide[:, experts : experts + 2].T.astype(jnp.float32)
    shifts = wide[:, experts + 2 : experts + 4].T.astype(jnp.float32)
    return (whole(0, 3 * width), whole(3 * width, base), wide[:, :experts], gains, shifts)


def owner_gates(incoming, router_full):
    logits = jnp.einsum("sjcd,de->sjce", incoming, router_full, preferred_element_type=jnp.float32)
    router_probs, _ = softmax_rows(logits)
    local = incoming.shape[1]
    own = lax.axis_index("expert") * local + jnp.arange(local, dtype=jnp.int32)
    labels = jnp.arange(router_full.shape[1], dtype=jnp.int32)
    pick = (own[:, None] == labels[None, :]).astype(jnp.float32)
    return jnp.sum(router_probs * pick[None, :, None, :], axis=-1, keepdims=True)


def gather_experts(which, w_first, w_second):
    if which == 0:
        both = jnp.stack([jnp.swapaxes(w_first[which], 1, 2), w_second[which]])
        both = lax.all_gather(both, "dp", axis=2, tiled=True)
        return (both[0], both[1])
    first_full = lax.all_gather(w_first[which], "dp", axis=2, tiled=True)
    second_full = lax.all_gather(w_second[which], "dp", axis=1, tiled=True)
    return (jnp.swapaxes(first_full, 1, 2), second_full)


def route_tables(route, experts_total, capacity):
    labels = jnp.arange(experts_total, dtype=jnp.int32)
    pick_first = (route[:, 0:1] == labels[None, :]).astype(jnp.int32)
    pick_second = (route[:, 1:2] == labels[None, :]).astype(jnp.int32)
    both_picks = pick_first + pick_second
    before = jnp.cumsum(both_picks, axis=0) - both_picks
    slot_first = route[:, 0] * capacity + jnp.sum(before * pick_first, axis=1)
    slot_second = route[:, 1] * capacity + jnp.sum(before * pick_second, axis=1)
    slot_ids = jnp.arange(experts_total * capacity, dtype=jnp.int32)
    place_first = (slot_ids[:, None] == slot_first[None, :]).astype(jnp.bfloat16)
    place_second = (slot_ids[:, None] == slot_second[None, :]).astype(jnp.bfloat16)
    return (
        pick_first.astype(jnp.float32),
        pick_second.astype(jnp.float32),
        place_first,
        place_second,
    )


def exchange(block):
    return lax.all_to_all(block, "expert", split_axis=0, concat_axis=0, tiled=True)


def head_of(ref, part, head):
    start = part * HEADS * HEAD_DIM + head * HEAD_DIM
    return ref[:, start : start + HEAD_DIM]


def masked_scores(query, keyed):
    scores = lax.dot_general(query, keyed, ROW_DOTS, preferred_element_type=jnp.float32)
    columns = lax.broadcasted_iota(jnp.int32, scores.shape, 1)
    return jnp.where(columns < SEQ, scores, -1e30)


def attention_kernel(packed_ref, mixed_ref, total_ref):
    scale = jnp.asarray(HEAD_DIM ** (-0.5), jnp.bfloat16)
    mixed, totals = [], []
    for head in range(HEADS):
        query = head_of(packed_ref, 0, head) * scale
        scores = masked_scores(query, head_of(packed_ref, 1, head))
        highest = jnp.max(scores, axis=-1, keepdims=True)
        powers = jnp.exp(scores - highest)
        row_total = jnp.sum(powers, axis=-1, keepdims=True)
        probs = (powers * (1.0 / row_total)).astype(jnp.bfloat16)
        mixed.append(
            jnp.dot(
                probs, head_of(packed_ref, 2, head), preferred_element_type=jnp.float32
            ).astype(jnp.bfloat16)
        )
        totals.append(highest + jnp.log(row_total))
    mixed_ref[...] = jnp.concatenate(mixed, axis=1)
    total_ref[...] = jnp.concatenate(totals, axis=1)


def attention_back_kernel(packed_ref, grad_ref, total_ref, out_ref):
    scale = jnp.asarray(HEAD_DIM ** (-0.5), jnp.bfloat16)
    queries, keys, values = [], [], []
    for head in range(HEADS):
        query = head_of(packed_ref, 0, head) * scale
        keyed = head_of(packed_ref, 1, head)
        grad_mixed = head_of(grad_ref, 0, head)
        scores = masked_scores(query, keyed)
        probs = jnp.exp(scores - total_ref[:, head : head + 1])
        grad_probs = lax.dot_general(
            grad_mixed,
            head_of(packed_ref, 2, head),
            ROW_DOTS,
            preferred_element_type=jnp.float32,
        )
        values.append(
            lax.dot_general(
                probs.astype(jnp.bfloat16),
                grad_mixed,
                COL_DOTS,
                preferred_element_type=jnp.float32,
            ).astype(jnp.bfloat16)
        )
        row_inner = jnp.sum(probs * grad_probs, axis=-1, keepdims=True)
        grad_scores = (probs * (grad_probs - row_inner)).astype(jnp.bfloat16)
        grad_query = jnp.dot(grad_scores, keyed, preferred_element_type=jnp.float32)
        queries.append(grad_query.astype(jnp.bfloat16) * scale)
        keys.append(
            lax.dot_general(
                grad_scores, query, COL_DOTS, preferred_element_type=jnp.float32
            ).astype(jnp.bfloat16)
        )
    out_ref[...] = jnp.concatenate(queries + keys + values, axis=1)


def image_block(columns):
    return pl.BlockSpec((SEQ_PAD, columns), lambda image: (image, 0))


def attention(packed):
    rows, columns = packed.shape
    width = columns // 3
    return pl.pallas_call(
        attention_kernel,
        grid=(rows // SEQ_PAD,),
        in_specs=[image_block(columns)],
        out_specs=[image_block(width), image_block(HEADS)],
        out_shape=[
            jax.ShapeDtypeStruct((rows, width), jnp.bfloat16),
            jax.ShapeDtypeStruct((rows, HEADS), jnp.float32),
        ],
        name="attention",
    )(packed)


def attention_back(packed, grad_mixed, totals):
    rows, columns = packed.shape
    return pl.pallas_call(
        attention_back_kernel,
        grid=(rows // SEQ_PAD,),
        in_specs=[image_block(columns), image_block(columns // 3), image_block(HEADS)],
        out_specs=image_block(columns),
        out_shape=jax.ShapeDtypeStruct((rows, columns), jnp.bfloat16),
        name="attention_back",
    )(packed, grad_mixed, totals)


def attend_forward(resid, dense, tables):
    qkv_full, proj_full, router_full, gains_wide, shifts_wide = dense
    pick_first_f, pick_second_f, _, _ = tables
    attn_norm, unit_a, inv_a = layer_norm(resid, gains_wide[0], shifts_wide[0])
    attn_in = attn_norm.astype(jnp.bfloat16)
    packed = jnp.dot(attn_in, qkv_full, preferred_element_type=jnp.float32)
    packed = packed.astype(jnp.bfloat16)
    mixed, totals = attention(packed)
    resid_mid = resid + jnp.dot(mixed, proj_full, preferred_element_type=jnp.float32)
    moe_norm, unit_b, inv_b = layer_norm(resid_mid, gains_wide[1], shifts_wide[1])
    moe_in = moe_norm.astype(jnp.bfloat16)
    logits = jnp.dot(moe_in, router_full, preferred_element_type=jnp.float32)
    router_probs, _ = softmax_rows(logits)
    gate_first = jnp.sum(router_probs * pick_first_f, axis=1)
    gate_second = jnp.sum(router_probs * pick_second_f, axis=1)
    router_probs, gate_first, gate_second = lax.optimization_barrier(
        (router_probs, gate_first, gate_second)
    )
    attn_saved = (unit_a, inv_a, attn_in, packed, totals, mixed)
    moe_saved = (unit_b, inv_b, moe_in, router_probs, gate_first, gate_second)
    return (resid_mid, attn_saved, moe_saved)


def slots_of(rows, place, block_shape):
    slots = jnp.dot(place, rows, preferred_element_type=jnp.float32)
    return slots.astype(jnp.bfloat16).reshape(block_shape)


def gated_slots(grad_out, moe_saved, tables, block_shape):
    gate_first, gate_second = moe_saved[4:]
    place_first, place_second = tables[2:]
    send_first = (gate_first[:, None] * grad_out).astype(jnp.bfloat16)
    send_second = (gate_second[:, None] * grad_out).astype(jnp.bfloat16)
    slots = jnp.dot(place_first, send_first, preferred_element_type=jnp.float32) + jnp.dot(
        place_second, send_second, preferred_element_type=jnp.float32
    )
    return slots.astype(jnp.bfloat16).reshape(block_shape)


def experts_hidden(incoming, first_full):
    hidden_pre = jnp.einsum(
        "sjcd,jfd->sjcf", incoming, first_full, preferred_element_type=jnp.float32
    )
    return (hidden_pre, gelu_value(hidden_pre).astype(jnp.bfloat16))


def experts_result(hidden_act, second_full):
    return jnp.einsum(
        "sjcf,jfd->sjcd", hidden_act, second_full, preferred_element_type=jnp.float32
    ).astype(jnp.bfloat16)


def rows_back(returned, place):
    return jnp.einsum("st,sd->td", place, returned, preferred_element_type=jnp.float32)


def experts_backward(grad_result, incoming, hidden_pre, hidden_act, experts):
    first_full, second_full = experts
    grad_second = jnp.einsum(
        "sjcf,sjcd->jfd", hidden_act, grad_result, preferred_element_type=jnp.float32
    ).astype(jnp.bfloat16)
    share_second = lax.psum_scatter(grad_second, "dp", scatter_dimension=1, tiled=True)
    grad_act = jnp.einsum(
        "sjcd,jfd->sjcf", grad_result, second_full, preferred_element_type=jnp.float32
    )
    grad_pre = (grad_act * gelu_slope(hidden_pre)).astype(jnp.bfloat16)
    grad_rows = jnp.einsum(
        "sjcf,jfd->sjcd", grad_pre, first_full, preferred_element_type=jnp.float32
    ).astype(jnp.bfloat16)
    grad_back = exchange(grad_rows)
    grad_first = jnp.einsum(
        "sjcd,sjcf->jdf", incoming, grad_pre, preferred_element_type=jnp.float32
    ).astype(jnp.bfloat16)
    grad_back, grad_first = lax.optimization_barrier((grad_back, grad_first))
    share_first = lax.psum_scatter(grad_first, "dp", scatter_dimension=2, tiled=True)
    return (grad_back, share_first, share_second)


def tokens_backward(grad_out, grad_back, backs, dense, tables, attn_saved, moe_saved):
    qkv_full, proj_full, router_full, gains_wide, _ = dense
    pick_first_f, pick_second_f, place_first, place_second = tables
    unit_a, inv_a, attn_in, packed, totals, mixed = attn_saved
    unit_b, inv_b, moe_in, router_probs, _, _ = moe_saved
    width = grad_out.shape[1]
    grad_gate_first = jnp.sum(grad_out * backs[0], axis=1)
    grad_gate_second = jnp.sum(grad_out * backs[1], axis=1)
    grad_back = grad_back.reshape(-1, width)
    grad_moe = rows_back(grad_back, place_first + place_second)
    grad_probs = pick_first_f * grad_gate_first[:, None] + pick_second_f * grad_gate_second[:, None]
    weighted = jnp.sum(router_probs * grad_probs, axis=1, keepdims=True)
    grad_logits = (router_probs * (grad_probs - weighted)).astype(jnp.bfloat16)
    grad_router = jnp.einsum("td,te->de", moe_in, grad_logits, preferred_element_type=jnp.float32)
    grad_moe = grad_moe + jnp.einsum(
        "te,de->td", grad_logits, router_full, preferred_element_type=jnp.float32
    )
    grad_norm_b, gain_b_grad, shift_b_grad = norm_back(grad_moe, unit_b, inv_b, gains_wide[1])
    grad_mid = grad_out + grad_norm_b
    grad_branch = grad_mid.astype(jnp.bfloat16)
    grad_proj = jnp.einsum("td,te->de", mixed, grad_branch, preferred_element_type=jnp.float32)
    grad_mixed = jnp.einsum("te,de->td", grad_branch, proj_full, preferred_element_type=jnp.float32)
    grad_packed = attention_back(packed, grad_mixed.astype(jnp.bfloat16), totals)
    grad_qkv = jnp.einsum("td,te->de", attn_in, grad_packed, preferred_element_type=jnp.float32)
    grad_attn = jnp.einsum("te,de->td", grad_packed, qkv_full, preferred_element_type=jnp.float32)
    grad_norm_a, gain_a_grad, shift_a_grad = norm_back(grad_attn, unit_a, inv_a, gains_wide[0])
    grad_in = grad_mid + grad_norm_a
    low = jnp.bfloat16
    small = jnp.concatenate(
        [
            grad_qkv.astype(low),
            grad_proj.astype(low),
            grad_router.astype(low),
            jnp.stack([gain_a_grad, gain_b_grad, shift_a_grad, shift_b_grad], axis=1).astype(low),
        ],
        axis=1,
    )
    peers, shares = lax.axis_size("expert"), lax.axis_size("dp")
    piece = width // (peers * shares)
    columns = small.shape[1]
    small = small.reshape(shares, peers, piece, columns).swapaxes(0, 1)
    return (grad_in, small)


def sum_small(small):
    small = exchange(small)
    return jnp.sum(small.astype(jnp.float32), axis=0).astype(jnp.bfloat16)


def whole_step(
    embedded, cotangent, w_qkv, w_proj, w_router, norm_gains, norm_shifts, w_first, w_second, routes
):
    images, length, width = embedded.shape
    tok_count = images * length
    experts_total = w_router.shape[2]
    peers = lax.axis_size("expert")
    capacity = -(-max(2, 3 * tok_count // experts_total) // 8) * 8
    block_shape = (peers, experts_total // peers, capacity, width)
    fill = ((0, 0), (0, SEQ_PAD - length), (0, 0))
    rows = images * SEQ_PAD
    cot_low = jnp.pad(cotangent, fill).reshape(rows, width)
    resid = jnp.pad(embedded, fill).reshape(rows, width).astype(jnp.float32)
    grad = cot_low.astype(jnp.float32)
    dense, experts, tables = [], [], []
    quarters = gather_quarters(w_qkv, w_proj, w_router, norm_gains, norm_shifts)
    for which in range(LAYERS):
        experts.append(gather_experts(which, w_first, w_second))
        route = jnp.pad(routes[which], fill, constant_values=experts_total).reshape(rows, 2)
        tables.append(route_tables(route, experts_total, capacity))
    last = tables[LAYERS - 1]
    slots = slots_of(cot_low, last[2] + last[3], block_shape)
    cot_rows = exchange(slots)
    for which in range(LAYERS):
        dense.append(spread_dense(quarters[which], experts_total))
    attn_saved, moe_saved, kept = [], [], []
    grad_result = None
    for which in range(LAYERS):
        table = tables[which]
        resid_mid, attn_part, moe_part = attend_forward(resid, dense[which], table)
        outgoing = slots_of(moe_part[2], table[2] + table[3], block_shape)
        incoming = exchange(outgoing)
        hidden_pre, hidden_act = experts_hidden(incoming, experts[which][0])
        if which == LAYERS - 1:
            gates = owner_gates(incoming, dense[which][2])
            grad_result = (gates * cot_rows.astype(jnp.float32)).astype(jnp.bfloat16)
        result = experts_result(hidden_act, experts[which][1])
        returned = exchange(result).reshape(experts_total * capacity, width)
        backs = (rows_back(returned, table[2]), rows_back(returned, table[3]))
        resid = resid_mid + (
            moe_part[4][:, None] * backs[0] + moe_part[5][:, None] * backs[1]
        )
        attn_saved.append(attn_part)
        moe_saved.append(moe_part)
        kept.append((incoming, hidden_pre, hidden_act, backs))
    out_images = resid.reshape(images, SEQ_PAD, width)[:, :length].astype(jnp.bfloat16)
    smalls, firsts, seconds = [None] * LAYERS, [None] * LAYERS, [None] * LAYERS
    for which in reversed(range(LAYERS)):
        incoming, hidden_pre, hidden_act, backs = kept[which]
        if which < LAYERS - 1:
            slots = gated_slots(grad, moe_saved[which], tables[which], block_shape)
            grad_result = exchange(slots)
            grad_result, smalls[which + 1] = lax.optimization_barrier(
                (grad_result, smalls[which + 1])
            )
        grad_back, firsts[which], seconds[which] = experts_backward(
            grad_result, incoming, hidden_pre, hidden_act, experts[which]
        )
        grad, smalls[which] = tokens_backward(
            grad,
            grad_back,
            backs,
            dense[which],
            tables[which],
            attn_saved[which],
            moe_saved[which],
        )
    for which in reversed(range(LAYERS)):
        smalls[which] = sum_small(smalls[which])
    both = jnp.stack(smalls, axis=2)
    both = lax.psum_scatter(both, "dp", scatter_dimension=0, tiled=True)[0]
    total = lax.all_gather(both, "expert", axis=0, tiled=True)
    total = total.swapaxes(0, 1).astype(jnp.float32)
    grad_images = grad.reshape(images, SEQ_PAD, width)[:, :length]
    wide = total[:, :, 4 * width :]
    return (
        out_images,
        grad_images,
        total[:, :, : 3 * width],
        total[:, :, 3 * width : 4 * width],
        wide[:, :, :experts_total],
        jnp.swapaxes(wide[:, :, experts_total : experts_total + 2], 1, 2),
        jnp.swapaxes(wide[:, :, experts_total + 2 :], 1, 2),
        jnp.stack(firsts).astype(jnp.float32),
        jnp.stack(seconds).astype(jnp.float32),
    )


def solution(mesh):

    return jax.shard_map(
        whole_step,
        mesh=mesh,
        in_specs=(
            P(("dp", "expert"), None, None),
            P(("dp", "expert"), None, None),
            P(None, "dp", None),
            P(None, "dp", None),
            P(None, "dp", None),
            P(None, None, "dp"),
            P(None, None, "dp"),
            P(None, "expert", None, "dp"),
            P(None, "expert", "dp", None),
            P(None, ("dp", "expert"), None, None),
        ),
        out_specs=(
            P(("dp", "expert"), None, None),
            P(("dp", "expert"), None, None),
            P(None, "dp", None),
            P(None, "dp", None),
            P(None, "dp", None),
            P(None, None, "dp"),
            P(None, None, "dp"),
            P(None, "expert", None, "dp"),
            P(None, "expert", "dp", None),
        ),
        check_vma=False,
    )
```

```python
import jax
import jax.numpy as jnp
from jax import lax
from jax.experimental import pallas as pl
from jax.sharding import PartitionSpec as P

HEADS = 8
HEAD_DIM = 64
SEQ = 197
SEQ_PAD = 208
LAYERS = 2
ROW_DOTS = (((1,), (1,)), ((), ()))
COL_DOTS = (((0,), (0,)), ((), ()))


EPSILON = 1e-06
ROOT_HALF = 0.7071067811865476
INV_ROOT_TAU = 0.3989422804014327


def layer_norm(values, scale_in, shift_in):
    center = values - jnp.mean(values, axis=-1, keepdims=True)
    variance = jnp.mean(center * center, axis=-1, keepdims=True)
    inverse = lax.rsqrt(variance + EPSILON)
    normed = center * inverse
    return (normed * scale_in + shift_in, normed, inverse)


def norm_back(grad_out, normed, inverse, scale_in):
    grad_normed = grad_out * scale_in
    first_mean = jnp.mean(grad_normed, axis=-1, keepdims=True)
    second_mean = jnp.mean(grad_normed * normed, axis=-1, keepdims=True)
    grad_in = inverse * (grad_normed - first_mean - normed * second_mean)
    return (grad_in, jnp.sum(grad_out * normed, axis=0), jnp.sum(grad_out, axis=0))


def softmax_rows(scores):
    highest = jnp.max(scores, axis=-1, keepdims=True)
    powers = jnp.exp(scores - highest)
    row_total = jnp.sum(powers, axis=-1, keepdims=True)
    return (powers / row_total, highest + jnp.log(row_total))


def gelu_value(preact):
    return 0.5 * preact * (1.0 + lax.erf(preact * ROOT_HALF))


def gelu_slope(preact):
    return (
        0.5 * (1.0 + lax.erf(preact * ROOT_HALF))
        + preact * jnp.exp(-0.5 * preact * preact) * INV_ROOT_TAU
    )


def gather_quarters(w_qkv, w_proj, w_router, norm_gains, norm_shifts):
    peers, rank = lax.axis_size("expert"), lax.axis_index("expert")
    piece = w_qkv.shape[1] // peers
    packed = jnp.concatenate(
        [w_qkv, w_proj, w_router, jnp.swapaxes(norm_gains, 1, 2), jnp.swapaxes(norm_shifts, 1, 2)],
        axis=2,
    )
    packed = lax.dynamic_slice_in_dim(packed, rank * piece, piece, axis=1)
    return lax.all_gather(packed, "dp", axis=1, tiled=True)


def spread_dense(quarter, experts):
    peers, shares = lax.axis_size("expert"), lax.axis_size("dp")
    rows, columns = quarter.shape
    parts = exchange(jnp.broadcast_to(quarter[None], (peers, rows, columns)))
    width = peers * rows
    parts = parts.reshape(peers, shares, rows // shares, columns)

    def whole(start, stop):
        return parts[..., start:stop].swapaxes(0, 1).reshape(width, stop - start)

    base = 4 * width
    wide = whole(base, columns)
    gains = wide[:, experts : experts + 2].T.astype(jnp.float32)
    shifts = wide[:, experts + 2 : experts + 4].T.astype(jnp.float32)
    return (whole(0, 3 * width), whole(3 * width, base), wide[:, :experts], gains, shifts)


def owner_gates(incoming, router_full):
    logits = jnp.einsum("sjcd,de->sjce", incoming, router_full, preferred_element_type=jnp.float32)
    router_probs, _ = softmax_rows(logits)
    local = incoming.shape[1]
    own = lax.axis_index("expert") * local + jnp.arange(local, dtype=jnp.int32)
    labels = jnp.arange(router_full.shape[1], dtype=jnp.int32)
    pick = (own[:, None] == labels[None, :]).astype(jnp.float32)
    return jnp.sum(router_probs * pick[None, :, None, :], axis=-1, keepdims=True)


def gather_experts(which, w_first, w_second):
    if which == 0:
        both = jnp.stack([jnp.swapaxes(w_first[which], 1, 2), w_second[which]])
        both = lax.all_gather(both, "dp", axis=2, tiled=True)
        return (both[0], both[1])
    first_full = lax.all_gather(w_first[which], "dp", axis=2, tiled=True)
    second_full = lax.all_gather(w_second[which], "dp", axis=1, tiled=True)
    return (jnp.swapaxes(first_full, 1, 2), second_full)


def route_tables(route, experts_total, capacity):
    labels = jnp.arange(experts_total, dtype=jnp.int32)
    pick_first = (route[:, 0:1] == labels[None, :]).astype(jnp.int32)
    pick_second = (route[:, 1:2] == labels[None, :]).astype(jnp.int32)
    both_picks = pick_first + pick_second
    before = jnp.cumsum(both_picks, axis=0) - both_picks
    slot_first = route[:, 0] * capacity + jnp.sum(before * pick_first, axis=1)
    slot_second = route[:, 1] * capacity + jnp.sum(before * pick_second, axis=1)
    slot_ids = jnp.arange(experts_total * capacity, dtype=jnp.int32)
    place_first = (slot_ids[:, None] == slot_first[None, :]).astype(jnp.bfloat16)
    place_second = (slot_ids[:, None] == slot_second[None, :]).astype(jnp.bfloat16)
    return (
        pick_first.astype(jnp.float32),
        pick_second.astype(jnp.float32),
        place_first,
        place_second,
    )


def exchange(block):
    return lax.all_to_all(block, "expert", split_axis=0, concat_axis=0, tiled=True)


def head_of(ref, part, head):
    start = part * HEADS * HEAD_DIM + head * HEAD_DIM
    return ref[:, start : start + HEAD_DIM]


def masked_scores(query, keyed):
    scores = lax.dot_general(query, keyed, ROW_DOTS, preferred_element_type=jnp.float32)
    columns = lax.broadcasted_iota(jnp.int32, scores.shape, 1)
    return jnp.where(columns < SEQ, scores, -1e30)


def attention_kernel(packed_ref, mixed_ref, total_ref):
    scale = jnp.asarray(HEAD_DIM ** (-0.5), jnp.bfloat16)
    mixed, totals = [], []
    for head in range(HEADS):
        query = head_of(packed_ref, 0, head) * scale
        scores = masked_scores(query, head_of(packed_ref, 1, head))
        highest = jnp.max(scores, axis=-1, keepdims=True)
        powers = jnp.exp(scores - highest)
        row_total = jnp.sum(powers, axis=-1, keepdims=True)
        probs = (powers * (1.0 / row_total)).astype(jnp.bfloat16)
        mixed.append(
            jnp.dot(
                probs, head_of(packed_ref, 2, head), preferred_element_type=jnp.float32
            ).astype(jnp.bfloat16)
        )
        totals.append(highest + jnp.log(row_total))
    mixed_ref[...] = jnp.concatenate(mixed, axis=1)
    total_ref[...] = jnp.concatenate(totals, axis=1)


def attention_back_kernel(packed_ref, grad_ref, total_ref, out_ref):
    scale = jnp.asarray(HEAD_DIM ** (-0.5), jnp.bfloat16)
    queries, keys, values = [], [], []
    for head in range(HEADS):
        query = head_of(packed_ref, 0, head) * scale
        keyed = head_of(packed_ref, 1, head)
        grad_mixed = head_of(grad_ref, 0, head)
        scores = masked_scores(query, keyed)
        probs = jnp.exp(scores - total_ref[:, head : head + 1])
        grad_probs = lax.dot_general(
            grad_mixed,
            head_of(packed_ref, 2, head),
            ROW_DOTS,
            preferred_element_type=jnp.float32,
        )
        values.append(
            lax.dot_general(
                probs.astype(jnp.bfloat16),
                grad_mixed,
                COL_DOTS,
                preferred_element_type=jnp.float32,
            ).astype(jnp.bfloat16)
        )
        row_inner = jnp.sum(probs * grad_probs, axis=-1, keepdims=True)
        grad_scores = (probs * (grad_probs - row_inner)).astype(jnp.bfloat16)
        grad_query = jnp.dot(grad_scores, keyed, preferred_element_type=jnp.float32)
        queries.append(grad_query.astype(jnp.bfloat16) * scale)
        keys.append(
            lax.dot_general(
                grad_scores, query, COL_DOTS, preferred_element_type=jnp.float32
            ).astype(jnp.bfloat16)
        )
    out_ref[...] = jnp.concatenate(queries + keys + values, axis=1)


def image_block(columns):
    return pl.BlockSpec((SEQ_PAD, columns), lambda image: (image, 0))


def attention(packed):
    rows, columns = packed.shape
    width = columns // 3
    return pl.pallas_call(
        attention_kernel,
        grid=(rows // SEQ_PAD,),
        in_specs=[image_block(columns)],
        out_specs=[image_block(width), image_block(HEADS)],
        out_shape=[
            jax.ShapeDtypeStruct((rows, width), jnp.bfloat16),
            jax.ShapeDtypeStruct((rows, HEADS), jnp.float32),
        ],
        name="attention",
    )(packed)


def attention_back(packed, grad_mixed, totals):
    rows, columns = packed.shape
    return pl.pallas_call(
        attention_back_kernel,
        grid=(rows // SEQ_PAD,),
        in_specs=[image_block(columns), image_block(columns // 3), image_block(HEADS)],
        out_specs=image_block(columns),
        out_shape=jax.ShapeDtypeStruct((rows, columns), jnp.bfloat16),
        name="attention_back",
    )(packed, grad_mixed, totals)


def attend_forward(resid, dense, tables):
    qkv_full, proj_full, router_full, gains_wide, shifts_wide = dense
    pick_first_f, pick_second_f, _, _ = tables
    attn_norm, unit_a, inv_a = layer_norm(resid, gains_wide[0], shifts_wide[0])
    attn_in = attn_norm.astype(jnp.bfloat16)
    packed = jnp.dot(attn_in, qkv_full, preferred_element_type=jnp.float32)
    packed = packed.astype(jnp.bfloat16)
    mixed, totals = attention(packed)
    resid_mid = resid + jnp.dot(mixed, proj_full, preferred_element_type=jnp.float32)
    moe_norm, unit_b, inv_b = layer_norm(resid_mid, gains_wide[1], shifts_wide[1])
    moe_in = moe_norm.astype(jnp.bfloat16)
    logits = jnp.dot(moe_in, router_full, preferred_element_type=jnp.float32)
    router_probs, _ = softmax_rows(logits)
    gate_first = jnp.sum(router_probs * pick_first_f, axis=1)
    gate_second = jnp.sum(router_probs * pick_second_f, axis=1)
    router_probs, gate_first, gate_second = lax.optimization_barrier(
        (router_probs, gate_first, gate_second)
    )
    attn_saved = (unit_a, inv_a, attn_in, packed, totals, mixed)
    moe_saved = (unit_b, inv_b, moe_in, router_probs, gate_first, gate_second)
    return (resid_mid, attn_saved, moe_saved)


def slots_of(rows, place, block_shape):
    slots = jnp.dot(place, rows, preferred_element_type=jnp.float32)
    return slots.astype(jnp.bfloat16).reshape(block_shape)


def gated_slots(grad_out, moe_saved, tables, block_shape):
    gate_first, gate_second = moe_saved[4:]
    place_first, place_second = tables[2:]
    send_first = (gate_first[:, None] * grad_out).astype(jnp.bfloat16)
    send_second = (gate_second[:, None] * grad_out).astype(jnp.bfloat16)
    slots = jnp.dot(place_first, send_first, preferred_element_type=jnp.float32) + jnp.dot(
        place_second, send_second, preferred_element_type=jnp.float32
    )
    return slots.astype(jnp.bfloat16).reshape(block_shape)


def experts_hidden(incoming, first_full):
    hidden_pre = jnp.einsum(
        "sjcd,jfd->sjcf", incoming, first_full, preferred_element_type=jnp.float32
    )
    return (hidden_pre, gelu_value(hidden_pre).astype(jnp.bfloat16))


def experts_result(hidden_act, second_full):
    return jnp.einsum(
        "sjcf,jfd->sjcd", hidden_act, second_full, preferred_element_type=jnp.float32
    ).astype(jnp.bfloat16)


def rows_back(returned, place):
    return jnp.einsum("st,sd->td", place, returned, preferred_element_type=jnp.float32)


def experts_backward(grad_result, incoming, hidden_pre, hidden_act, experts):
    first_full, second_full = experts
    grad_second = jnp.einsum(
        "sjcf,sjcd->jfd", hidden_act, grad_result, preferred_element_type=jnp.float32
    ).astype(jnp.bfloat16)
    share_second = lax.psum_scatter(grad_second, "dp", scatter_dimension=1, tiled=True)
    grad_act = jnp.einsum(
        "sjcd,jfd->sjcf", grad_result, second_full, preferred_element_type=jnp.float32
    )
    grad_pre = (grad_act * gelu_slope(hidden_pre)).astype(jnp.bfloat16)
    grad_rows = jnp.einsum(
        "sjcf,jfd->sjcd", grad_pre, first_full, preferred_element_type=jnp.float32
    ).astype(jnp.bfloat16)
    grad_back = exchange(grad_rows)
    grad_first = jnp.einsum(
        "sjcd,sjcf->jdf", incoming, grad_pre, preferred_element_type=jnp.float32
    ).astype(jnp.bfloat16)
    grad_back, grad_first = lax.optimization_barrier((grad_back, grad_first))
    share_first = lax.psum_scatter(grad_first, "dp", scatter_dimension=2, tiled=True)
    return (grad_back, share_first, share_second)


def tokens_backward(grad_out, grad_back, backs, dense, tables, attn_saved, moe_saved):
    qkv_full, proj_full, router_full, gains_wide, _ = dense
    pick_first_f, pick_second_f, place_first, place_second = tables
    unit_a, inv_a, attn_in, packed, totals, mixed = attn_saved
    unit_b, inv_b, moe_in, router_probs, _, _ = moe_saved
    width = grad_out.shape[1]
    grad_gate_first = jnp.sum(grad_out * backs[0], axis=1)
    grad_gate_second = jnp.sum(grad_out * backs[1], axis=1)
    grad_back = grad_back.reshape(-1, width)
    grad_moe = rows_back(grad_back, place_first + place_second)
    grad_probs = pick_first_f * grad_gate_first[:, None] + pick_second_f * grad_gate_second[:, None]
    weighted = jnp.sum(router_probs * grad_probs, axis=1, keepdims=True)
    grad_logits = (router_probs * (grad_probs - weighted)).astype(jnp.bfloat16)
    grad_router = jnp.einsum("td,te->de", moe_in, grad_logits, preferred_element_type=jnp.float32)
    grad_moe = grad_moe + jnp.einsum(
        "te,de->td", grad_logits, router_full, preferred_element_type=jnp.float32
    )
    grad_norm_b, gain_b_grad, shift_b_grad = norm_back(grad_moe, unit_b, inv_b, gains_wide[1])
    grad_mid = grad_out + grad_norm_b
    grad_branch = grad_mid.astype(jnp.bfloat16)
    grad_proj = jnp.einsum("td,te->de", mixed, grad_branch, preferred_element_type=jnp.float32)
    grad_mixed = jnp.einsum("te,de->td", grad_branch, proj_full, preferred_element_type=jnp.float32)
    grad_packed = attention_back(packed, grad_mixed.astype(jnp.bfloat16), totals)
    grad_qkv = jnp.einsum("td,te->de", attn_in, grad_packed, preferred_element_type=jnp.float32)
    grad_attn = jnp.einsum("te,de->td", grad_packed, qkv_full, preferred_element_type=jnp.float32)
    grad_norm_a, gain_a_grad, shift_a_grad = norm_back(grad_attn, unit_a, inv_a, gains_wide[0])
    grad_in = grad_mid + grad_norm_a
    low = jnp.bfloat16
    small = jnp.concatenate(
        [
            grad_qkv.astype(low),
            grad_proj.astype(low),
            grad_router.astype(low),
            jnp.stack([gain_a_grad, gain_b_grad, shift_a_grad, shift_b_grad], axis=1).astype(low),
        ],
        axis=1,
    )
    peers, chips = lax.axis_size("expert"), lax.axis_size("dp") // 2
    small = small.reshape(chips, 2, peers, width // (2 * chips * peers), small.shape[1])
    small = small.transpose(1, 2, 0, 3, 4)
    return (grad_in, small)


def halve(block, bit, step):
    size = lax.axis_size("dp")
    kept = lax.dynamic_index_in_dim(block, bit, 0, keepdims=False)
    sent = lax.dynamic_index_in_dim(block, 1 - bit, 0, keepdims=False)
    moved = lax.ppermute(sent, "dp", [(source, source ^ step) for source in range(size)])
    return (kept.astype(jnp.float32) + moved.astype(jnp.float32)).astype(jnp.bfloat16)


def sum_small(small):
    place = lax.axis_index("dp")
    small = halve(small, place % 2, 1)
    small = exchange(small)
    small = jnp.sum(small.astype(jnp.float32), axis=0).astype(jnp.bfloat16)
    step = 2
    while small.shape[0] > 1:
        chips, rows, columns = small.shape
        block = small.reshape(chips // 2, 2, rows, columns).swapaxes(0, 1)
        small = halve(block, (place // step) % 2, step)
        step = 2 * step
    return small[0]


def whole_step(
    embedded, cotangent, w_qkv, w_proj, w_router, norm_gains, norm_shifts, w_first, w_second, routes
):
    images, length, width = embedded.shape
    tok_count = images * length
    experts_total = w_router.shape[2]
    peers = lax.axis_size("expert")
    capacity = -(-max(2, 3 * tok_count // experts_total) // 8) * 8
    block_shape = (peers, experts_total // peers, capacity, width)
    fill = ((0, 0), (0, SEQ_PAD - length), (0, 0))
    rows = images * SEQ_PAD
    cot_low = jnp.pad(cotangent, fill).reshape(rows, width)
    resid = jnp.pad(embedded, fill).reshape(rows, width).astype(jnp.float32)
    grad = cot_low.astype(jnp.float32)
    dense, experts, tables = [], [], []
    quarters = gather_quarters(w_qkv, w_proj, w_router, norm_gains, norm_shifts)
    for which in range(LAYERS):
        experts.append(gather_experts(which, w_first, w_second))
        route = jnp.pad(routes[which], fill, constant_values=experts_total).reshape(rows, 2)
        tables.append(route_tables(route, experts_total, capacity))
    last = tables[LAYERS - 1]
    slots = slots_of(cot_low, last[2] + last[3], block_shape)
    cot_rows = exchange(slots)
    for which in range(LAYERS):
        dense.append(spread_dense(quarters[which], experts_total))
    attn_saved, moe_saved, kept = [], [], []
    grad_result = None
    for which in range(LAYERS):
        table = tables[which]
        resid_mid, attn_part, moe_part = attend_forward(resid, dense[which], table)
        outgoing = slots_of(moe_part[2], table[2] + table[3], block_shape)
        incoming = exchange(outgoing)
        hidden_pre, hidden_act = experts_hidden(incoming, experts[which][0])
        if which == LAYERS - 1:
            gates = owner_gates(incoming, dense[which][2])
            grad_result = (gates * cot_rows.astype(jnp.float32)).astype(jnp.bfloat16)
        result = experts_result(hidden_act, experts[which][1])
        returned = exchange(result).reshape(experts_total * capacity, width)
        backs = (rows_back(returned, table[2]), rows_back(returned, table[3]))
        resid = resid_mid + (
            moe_part[4][:, None] * backs[0] + moe_part[5][:, None] * backs[1]
        )
        attn_saved.append(attn_part)
        moe_saved.append(moe_part)
        kept.append((incoming, hidden_pre, hidden_act, backs))
    out_images = resid.reshape(images, SEQ_PAD, width)[:, :length].astype(jnp.bfloat16)
    smalls, firsts, seconds = [None] * LAYERS, [None] * LAYERS, [None] * LAYERS
    for which in reversed(range(LAYERS)):
        incoming, hidden_pre, hidden_act, backs = kept[which]
        if which < LAYERS - 1:
            slots = gated_slots(grad, moe_saved[which], tables[which], block_shape)
            grad_result = exchange(slots)
            grad_result, smalls[which + 1] = lax.optimization_barrier(
                (grad_result, smalls[which + 1])
            )
        grad_back, firsts[which], seconds[which] = experts_backward(
            grad_result, incoming, hidden_pre, hidden_act, experts[which]
        )
        grad, smalls[which] = tokens_backward(
            grad,
            grad_back,
            backs,
            dense[which],
            tables[which],
            attn_saved[which],
            moe_saved[which],
        )
    for which in reversed(range(LAYERS)):
        smalls[which] = sum_small(smalls[which])
    both = jnp.stack(smalls, axis=1)
    total = lax.all_gather(both, "expert", axis=0, tiled=True)
    total = total.swapaxes(0, 1).astype(jnp.float32)
    grad_images = grad.reshape(images, SEQ_PAD, width)[:, :length]
    wide = total[:, :, 4 * width :]
    return (
        out_images,
        grad_images,
        total[:, :, : 3 * width],
        total[:, :, 3 * width : 4 * width],
        wide[:, :, :experts_total],
        jnp.swapaxes(wide[:, :, experts_total : experts_total + 2], 1, 2),
        jnp.swapaxes(wide[:, :, experts_total + 2 :], 1, 2),
        jnp.stack(firsts).astype(jnp.float32),
        jnp.stack(seconds).astype(jnp.float32),
    )


def solution(mesh):

    return jax.shard_map(
        whole_step,
        mesh=mesh,
        in_specs=(
            P(("dp", "expert"), None, None),
            P(("dp", "expert"), None, None),
            P(None, "dp", None),
            P(None, "dp", None),
            P(None, "dp", None),
            P(None, None, "dp"),
            P(None, None, "dp"),
            P(None, "expert", None, "dp"),
            P(None, "expert", "dp", None),
            P(None, ("dp", "expert"), None, None),
        ),
        out_specs=(
            P(("dp", "expert"), None, None),
            P(("dp", "expert"), None, None),
            P(None, "dp", None),
            P(None, "dp", None),
            P(None, "dp", None),
            P(None, None, "dp"),
            P(None, None, "dp"),
            P(None, "expert", None, "dp"),
            P(None, "expert", "dp", None),
        ),
        check_vma=False,
    )
```

```python
import jax
import jax.numpy as jnp
from jax import lax
from jax.experimental import pallas as pl
from jax.sharding import PartitionSpec as P

HEADS = 8
HEAD_DIM = 64
SEQ = 197
SEQ_PAD = 208
LAYERS = 2
ROW_DOTS = (((1,), (1,)), ((), ()))
COL_DOTS = (((0,), (0,)), ((), ()))


EPSILON = 1e-06
ROOT_HALF = 0.7071067811865476
INV_ROOT_TAU = 0.3989422804014327


def layer_norm(values, scale_in, shift_in):
    center = values - jnp.mean(values, axis=-1, keepdims=True)
    variance = jnp.mean(center * center, axis=-1, keepdims=True)
    inverse = lax.rsqrt(variance + EPSILON)
    normed = center * inverse
    return (normed * scale_in + shift_in, normed, inverse)


def norm_back(grad_out, normed, inverse, scale_in):
    grad_normed = grad_out * scale_in
    first_mean = jnp.mean(grad_normed, axis=-1, keepdims=True)
    second_mean = jnp.mean(grad_normed * normed, axis=-1, keepdims=True)
    grad_in = inverse * (grad_normed - first_mean - normed * second_mean)
    return (grad_in, jnp.sum(grad_out * normed, axis=0), jnp.sum(grad_out, axis=0))


def softmax_rows(scores):
    highest = jnp.max(scores, axis=-1, keepdims=True)
    powers = jnp.exp(scores - highest)
    row_total = jnp.sum(powers, axis=-1, keepdims=True)
    return (powers / row_total, highest + jnp.log(row_total))


def gelu_value(preact):
    return 0.5 * preact * (1.0 + lax.erf(preact * ROOT_HALF))


def gelu_slope(preact):
    return (
        0.5 * (1.0 + lax.erf(preact * ROOT_HALF))
        + preact * jnp.exp(-0.5 * preact * preact) * INV_ROOT_TAU
    )


def gather_quarters(w_qkv, w_proj, w_router, norm_gains, norm_shifts):
    peers, rank = lax.axis_size("expert"), lax.axis_index("expert")
    piece = w_qkv.shape[1] // peers
    packed = jnp.concatenate(
        [w_qkv, w_proj, w_router, jnp.swapaxes(norm_gains, 1, 2), jnp.swapaxes(norm_shifts, 1, 2)],
        axis=2,
    )
    block = lax.dynamic_slice_in_dim(packed, rank * piece, piece, axis=1)[None]
    place, size, step = lax.axis_index("dp"), lax.axis_size("dp"), 2
    while step < size:
        moved = lax.ppermute(block, "dp", [(source, source ^ step) for source in range(size)])
        upper = (place // step) % 2 == 1
        first, second = jnp.where(upper, moved, block), jnp.where(upper, block, moved)
        block = jnp.concatenate([first, second], axis=0)
        step = 2 * step
    return block


def spread_quarter(quarter):
    parts = jnp.broadcast_to(quarter[None], (lax.axis_size("expert"),) + quarter.shape)
    return exchange(parts)


def join_cores(parts, experts):
    size = lax.axis_size("dp")
    peers, chips, rows, columns = parts.shape
    other = lax.ppermute(parts, "dp", [(source, source ^ 1) for source in range(size)])
    core = lax.axis_index("dp") % 2
    width = 2 * peers * chips * rows
    own = lax.broadcasted_iota(jnp.int32, (1, 2, 1, 1, 1), 1) == core

    def whole(start, stop):
        mine = parts[..., start:stop].swapaxes(0, 1)[:, None]
        theirs = other[..., start:stop].swapaxes(0, 1)[:, None]
        return jnp.where(own, mine, theirs).reshape(width, stop - start)

    base = 4 * width
    wide = whole(base, columns)
    gains = wide[:, experts : experts + 2].T.astype(jnp.float32)
    shifts = wide[:, experts + 2 : experts + 4].T.astype(jnp.float32)
    return (whole(0, 3 * width), whole(3 * width, base), wide[:, :experts], gains, shifts)


def owner_gates(incoming, router_full):
    logits = jnp.einsum("sjcd,de->sjce", incoming, router_full, preferred_element_type=jnp.float32)
    router_probs, _ = softmax_rows(logits)
    local = incoming.shape[1]
    own = lax.axis_index("expert") * local + jnp.arange(local, dtype=jnp.int32)
    labels = jnp.arange(router_full.shape[1], dtype=jnp.int32)
    pick = (own[:, None] == labels[None, :]).astype(jnp.float32)
    return jnp.sum(router_probs * pick[None, :, None, :], axis=-1, keepdims=True)


def gather_experts(which, w_first, w_second):
    if which == 0:
        both = jnp.stack([jnp.swapaxes(w_first[which], 1, 2), w_second[which]])
        both = lax.all_gather(both, "dp", axis=2, tiled=True)
        return (both[0], both[1])
    first_full = lax.all_gather(w_first[which], "dp", axis=2, tiled=True)
    second_full = lax.all_gather(w_second[which], "dp", axis=1, tiled=True)
    return (jnp.swapaxes(first_full, 1, 2), second_full)


def route_tables(route, experts_total, capacity):
    labels = jnp.arange(experts_total, dtype=jnp.int32)
    pick_first = (route[:, 0:1] == labels[None, :]).astype(jnp.int32)
    pick_second = (route[:, 1:2] == labels[None, :]).astype(jnp.int32)
    both_picks = pick_first + pick_second
    before = jnp.cumsum(both_picks, axis=0) - both_picks
    slot_first = route[:, 0] * capacity + jnp.sum(before * pick_first, axis=1)
    slot_second = route[:, 1] * capacity + jnp.sum(before * pick_second, axis=1)
    slot_ids = jnp.arange(experts_total * capacity, dtype=jnp.int32)
    place_first = (slot_ids[:, None] == slot_first[None, :]).astype(jnp.bfloat16)
    place_second = (slot_ids[:, None] == slot_second[None, :]).astype(jnp.bfloat16)
    return (
        pick_first.astype(jnp.float32),
        pick_second.astype(jnp.float32),
        place_first,
        place_second,
    )


def exchange(block):
    return lax.all_to_all(block, "expert", split_axis=0, concat_axis=0, tiled=True)


def head_of(ref, part, head):
    start = part * HEADS * HEAD_DIM + head * HEAD_DIM
    return ref[:, start : start + HEAD_DIM]


def masked_scores(query, keyed):
    scores = lax.dot_general(query, keyed, ROW_DOTS, preferred_element_type=jnp.float32)
    columns = lax.broadcasted_iota(jnp.int32, scores.shape, 1)
    return jnp.where(columns < SEQ, scores, -1e30)


def attention_kernel(packed_ref, mixed_ref, total_ref):
    scale = jnp.asarray(HEAD_DIM ** (-0.5), jnp.bfloat16)
    mixed, totals = [], []
    for head in range(HEADS):
        query = head_of(packed_ref, 0, head) * scale
        scores = masked_scores(query, head_of(packed_ref, 1, head))
        highest = jnp.max(scores, axis=-1, keepdims=True)
        powers = jnp.exp(scores - highest)
        row_total = jnp.sum(powers, axis=-1, keepdims=True)
        probs = (powers * (1.0 / row_total)).astype(jnp.bfloat16)
        mixed.append(
            jnp.dot(
                probs, head_of(packed_ref, 2, head), preferred_element_type=jnp.float32
            ).astype(jnp.bfloat16)
        )
        totals.append(highest + jnp.log(row_total))
    mixed_ref[...] = jnp.concatenate(mixed, axis=1)
    total_ref[...] = jnp.concatenate(totals, axis=1)


def attention_back_kernel(packed_ref, grad_ref, total_ref, out_ref):
    scale = jnp.asarray(HEAD_DIM ** (-0.5), jnp.bfloat16)
    queries, keys, values = [], [], []
    for head in range(HEADS):
        query = head_of(packed_ref, 0, head) * scale
        keyed = head_of(packed_ref, 1, head)
        grad_mixed = head_of(grad_ref, 0, head)
        scores = masked_scores(query, keyed)
        probs = jnp.exp(scores - total_ref[:, head : head + 1])
        grad_probs = lax.dot_general(
            grad_mixed,
            head_of(packed_ref, 2, head),
            ROW_DOTS,
            preferred_element_type=jnp.float32,
        )
        values.append(
            lax.dot_general(
                probs.astype(jnp.bfloat16),
                grad_mixed,
                COL_DOTS,
                preferred_element_type=jnp.float32,
            ).astype(jnp.bfloat16)
        )
        row_inner = jnp.sum(probs * grad_probs, axis=-1, keepdims=True)
        grad_scores = (probs * (grad_probs - row_inner)).astype(jnp.bfloat16)
        grad_query = jnp.dot(grad_scores, keyed, preferred_element_type=jnp.float32)
        queries.append(grad_query.astype(jnp.bfloat16) * scale)
        keys.append(
            lax.dot_general(
                grad_scores, query, COL_DOTS, preferred_element_type=jnp.float32
            ).astype(jnp.bfloat16)
        )
    out_ref[...] = jnp.concatenate(queries + keys + values, axis=1)


def image_block(columns):
    return pl.BlockSpec((SEQ_PAD, columns), lambda image: (image, 0))


def attention(packed):
    rows, columns = packed.shape
    width = columns // 3
    return pl.pallas_call(
        attention_kernel,
        grid=(rows // SEQ_PAD,),
        in_specs=[image_block(columns)],
        out_specs=[image_block(width), image_block(HEADS)],
        out_shape=[
            jax.ShapeDtypeStruct((rows, width), jnp.bfloat16),
            jax.ShapeDtypeStruct((rows, HEADS), jnp.float32),
        ],
        name="attention",
    )(packed)


def attention_back(packed, grad_mixed, totals):
    rows, columns = packed.shape
    return pl.pallas_call(
        attention_back_kernel,
        grid=(rows // SEQ_PAD,),
        in_specs=[image_block(columns), image_block(columns // 3), image_block(HEADS)],
        out_specs=image_block(columns),
        out_shape=jax.ShapeDtypeStruct((rows, columns), jnp.bfloat16),
        name="attention_back",
    )(packed, grad_mixed, totals)


def attend_forward(resid, dense, tables):
    qkv_full, proj_full, router_full, gains_wide, shifts_wide = dense
    pick_first_f, pick_second_f, _, _ = tables
    attn_norm, unit_a, inv_a = layer_norm(resid, gains_wide[0], shifts_wide[0])
    attn_in = attn_norm.astype(jnp.bfloat16)
    packed = jnp.dot(attn_in, qkv_full, preferred_element_type=jnp.float32)
    packed = packed.astype(jnp.bfloat16)
    mixed, totals = attention(packed)
    resid_mid = resid + jnp.dot(mixed, proj_full, preferred_element_type=jnp.float32)
    moe_norm, unit_b, inv_b = layer_norm(resid_mid, gains_wide[1], shifts_wide[1])
    moe_in = moe_norm.astype(jnp.bfloat16)
    logits = jnp.dot(moe_in, router_full, preferred_element_type=jnp.float32)
    router_probs, _ = softmax_rows(logits)
    gate_first = jnp.sum(router_probs * pick_first_f, axis=1)
    gate_second = jnp.sum(router_probs * pick_second_f, axis=1)
    router_probs, gate_first, gate_second = lax.optimization_barrier(
        (router_probs, gate_first, gate_second)
    )
    attn_saved = (unit_a, inv_a, attn_in, packed, totals, mixed)
    moe_saved = (unit_b, inv_b, moe_in, router_probs, gate_first, gate_second)
    return (resid_mid, attn_saved, moe_saved)


def slots_of(rows, place, block_shape):
    slots = jnp.dot(place, rows, preferred_element_type=jnp.float32)
    return slots.astype(jnp.bfloat16).reshape(block_shape)


def gated_slots(grad_out, moe_saved, tables, block_shape):
    gate_first, gate_second = moe_saved[4:]
    place_first, place_second = tables[2:]
    send_first = (gate_first[:, None] * grad_out).astype(jnp.bfloat16)
    send_second = (gate_second[:, None] * grad_out).astype(jnp.bfloat16)
    slots = jnp.dot(place_first, send_first, preferred_element_type=jnp.float32) + jnp.dot(
        place_second, send_second, preferred_element_type=jnp.float32
    )
    return slots.astype(jnp.bfloat16).reshape(block_shape)


def experts_hidden(incoming, first_full):
    hidden_pre = jnp.einsum(
        "sjcd,jfd->sjcf", incoming, first_full, preferred_element_type=jnp.float32
    )
    return (hidden_pre, gelu_value(hidden_pre).astype(jnp.bfloat16))


def experts_result(hidden_act, second_full):
    return jnp.einsum(
        "sjcf,jfd->sjcd", hidden_act, second_full, preferred_element_type=jnp.float32
    ).astype(jnp.bfloat16)


def rows_back(returned, place):
    return jnp.einsum("st,sd->td", place, returned, preferred_element_type=jnp.float32)


def experts_backward(grad_result, incoming, hidden_pre, hidden_act, experts):
    first_full, second_full = experts
    grad_second = jnp.einsum(
        "sjcf,sjcd->jfd", hidden_act, grad_result, preferred_element_type=jnp.float32
    ).astype(jnp.bfloat16)
    share_second = lax.psum_scatter(grad_second, "dp", scatter_dimension=1, tiled=True)
    grad_act = jnp.einsum(
        "sjcd,jfd->sjcf", grad_result, second_full, preferred_element_type=jnp.float32
    )
    grad_pre = (grad_act * gelu_slope(hidden_pre)).astype(jnp.bfloat16)
    grad_rows = jnp.einsum(
        "sjcf,jfd->sjcd", grad_pre, first_full, preferred_element_type=jnp.float32
    ).astype(jnp.bfloat16)
    grad_back = exchange(grad_rows)
    grad_first = jnp.einsum(
        "sjcd,sjcf->jdf", incoming, grad_pre, preferred_element_type=jnp.float32
    ).astype(jnp.bfloat16)
    grad_back, grad_first = lax.optimization_barrier((grad_back, grad_first))
    share_first = lax.psum_scatter(grad_first, "dp", scatter_dimension=2, tiled=True)
    return (grad_back, share_first, share_second)


def tokens_backward(grad_out, grad_back, backs, dense, tables, attn_saved, moe_saved):
    qkv_full, proj_full, router_full, gains_wide, _ = dense
    pick_first_f, pick_second_f, place_first, place_second = tables
    unit_a, inv_a, attn_in, packed, totals, mixed = attn_saved
    unit_b, inv_b, moe_in, router_probs, _, _ = moe_saved
    width = grad_out.shape[1]
    grad_gate_first = jnp.sum(grad_out * backs[0], axis=1)
    grad_gate_second = jnp.sum(grad_out * backs[1], axis=1)
    grad_back = grad_back.reshape(-1, width)
    grad_moe = rows_back(grad_back, place_first + place_second)
    grad_probs = pick_first_f * grad_gate_first[:, None] + pick_second_f * grad_gate_second[:, None]
    weighted = jnp.sum(router_probs * grad_probs, axis=1, keepdims=True)
    grad_logits = (router_probs * (grad_probs - weighted)).astype(jnp.bfloat16)
    grad_router = jnp.einsum("td,te->de", moe_in, grad_logits, preferred_element_type=jnp.float32)
    grad_moe = grad_moe + jnp.einsum(
        "te,de->td", grad_logits, router_full, preferred_element_type=jnp.float32
    )
    grad_norm_b, gain_b_grad, shift_b_grad = norm_back(grad_moe, unit_b, inv_b, gains_wide[1])
    grad_mid = grad_out + grad_norm_b
    grad_branch = grad_mid.astype(jnp.bfloat16)
    grad_proj = jnp.einsum("td,te->de", mixed, grad_branch, preferred_element_type=jnp.float32)
    grad_mixed = jnp.einsum("te,de->td", grad_branch, proj_full, preferred_element_type=jnp.float32)
    grad_packed = attention_back(packed, grad_mixed.astype(jnp.bfloat16), totals)
    grad_qkv = jnp.einsum("td,te->de", attn_in, grad_packed, preferred_element_type=jnp.float32)
    grad_attn = jnp.einsum("te,de->td", grad_packed, qkv_full, preferred_element_type=jnp.float32)
    grad_norm_a, gain_a_grad, shift_a_grad = norm_back(grad_attn, unit_a, inv_a, gains_wide[0])
    grad_in = grad_mid + grad_norm_a
    low = jnp.bfloat16
    small = jnp.concatenate(
        [
            grad_qkv.astype(low),
            grad_proj.astype(low),
            grad_router.astype(low),
            jnp.stack([gain_a_grad, gain_b_grad, shift_a_grad, shift_b_grad], axis=1).astype(low),
        ],
        axis=1,
    )
    peers, chips = lax.axis_size("expert"), lax.axis_size("dp") // 2
    small = small.reshape(chips, 2, peers, width // (2 * chips * peers), small.shape[1])
    small = small.transpose(1, 2, 0, 3, 4)
    return (grad_in, small)


def halve(block, bit, step):
    size = lax.axis_size("dp")
    kept = lax.dynamic_index_in_dim(block, bit, 0, keepdims=False)
    sent = lax.dynamic_index_in_dim(block, 1 - bit, 0, keepdims=False)
    moved = lax.ppermute(sent, "dp", [(source, source ^ step) for source in range(size)])
    return (kept.astype(jnp.float32) + moved.astype(jnp.float32)).astype(jnp.bfloat16)


def sum_small(small):
    place = lax.axis_index("dp")
    small = halve(small, place % 2, 1)
    small = exchange(small)
    small = jnp.sum(small.astype(jnp.float32), axis=0).astype(jnp.bfloat16)
    step = 2
    while small.shape[0] > 1:
        chips, rows, columns = small.shape
        block = small.reshape(chips // 2, 2, rows, columns).swapaxes(0, 1)
        small = halve(block, (place // step) % 2, step)
        step = 2 * step
    return small[0]


def whole_step(
    embedded, cotangent, w_qkv, w_proj, w_router, norm_gains, norm_shifts, w_first, w_second, routes
):
    images, length, width = embedded.shape
    tok_count = images * length
    experts_total = w_router.shape[2]
    peers = lax.axis_size("expert")
    capacity = -(-max(2, 3 * tok_count // experts_total) // 8) * 8
    block_shape = (peers, experts_total // peers, capacity, width)
    fill = ((0, 0), (0, SEQ_PAD - length), (0, 0))
    rows = images * SEQ_PAD
    cot_low = jnp.pad(cotangent, fill).reshape(rows, width)
    resid = jnp.pad(embedded, fill).reshape(rows, width).astype(jnp.float32)
    grad = cot_low.astype(jnp.float32)
    dense, experts, tables = [], [], []
    quarters = gather_quarters(w_qkv, w_proj, w_router, norm_gains, norm_shifts)
    for which in range(LAYERS):
        experts.append(gather_experts(which, w_first, w_second))
        route = jnp.pad(routes[which], fill, constant_values=experts_total).reshape(rows, 2)
        tables.append(route_tables(route, experts_total, capacity))
    last = tables[LAYERS - 1]
    slots = slots_of(cot_low, last[2] + last[3], block_shape)
    cot_rows = exchange(slots)
    parts = []
    for which in range(LAYERS):
        parts.append(spread_quarter(quarters[:, which]))
    dense.append(join_cores(parts[0], experts_total))
    attn_saved, moe_saved, kept = [], [], []
    grad_result = None
    for which in range(LAYERS):
        table = tables[which]
        resid_mid, attn_part, moe_part = attend_forward(resid, dense[which], table)
        if which < LAYERS - 1:
            parts[which + 1], resid_mid = lax.optimization_barrier((parts[which + 1], resid_mid))
            dense.append(join_cores(parts[which + 1], experts_total))
        outgoing = slots_of(moe_part[2], table[2] + table[3], block_shape)
        incoming = exchange(outgoing)
        hidden_pre, hidden_act = experts_hidden(incoming, experts[which][0])
        if which == LAYERS - 1:
            gates = owner_gates(incoming, dense[which][2])
            grad_result = (gates * cot_rows.astype(jnp.float32)).astype(jnp.bfloat16)
        result = experts_result(hidden_act, experts[which][1])
        returned = exchange(result).reshape(experts_total * capacity, width)
        backs = (rows_back(returned, table[2]), rows_back(returned, table[3]))
        resid = resid_mid + (
            moe_part[4][:, None] * backs[0] + moe_part[5][:, None] * backs[1]
        )
        attn_saved.append(attn_part)
        moe_saved.append(moe_part)
        kept.append((incoming, hidden_pre, hidden_act, backs))
    out_images = resid.reshape(images, SEQ_PAD, width)[:, :length].astype(jnp.bfloat16)
    smalls, firsts, seconds = [None] * LAYERS, [None] * LAYERS, [None] * LAYERS
    for which in reversed(range(LAYERS)):
        incoming, hidden_pre, hidden_act, backs = kept[which]
        if which < LAYERS - 1:
            slots = gated_slots(grad, moe_saved[which], tables[which], block_shape)
            grad_result = exchange(slots)
            grad_result, smalls[which + 1] = lax.optimization_barrier(
                (grad_result, smalls[which + 1])
            )
        grad_back, firsts[which], seconds[which] = experts_backward(
            grad_result, incoming, hidden_pre, hidden_act, experts[which]
        )
        grad, smalls[which] = tokens_backward(
            grad,
            grad_back,
            backs,
            dense[which],
            tables[which],
            attn_saved[which],
            moe_saved[which],
        )
    for which in reversed(range(LAYERS)):
        smalls[which] = sum_small(smalls[which])
    both = jnp.stack(smalls, axis=1)
    grad_first = jnp.stack(firsts).astype(jnp.float32)
    grad_second = jnp.stack(seconds).astype(jnp.float32)
    both, grad_first, grad_second = lax.optimization_barrier((both, grad_first, grad_second))
    total = lax.all_gather(both, "expert", axis=0, tiled=True)
    total = total.swapaxes(0, 1).astype(jnp.float32)
    grad_images = grad.reshape(images, SEQ_PAD, width)[:, :length]
    wide = total[:, :, 4 * width :]
    return (
        out_images,
        grad_images,
        total[:, :, : 3 * width],
        total[:, :, 3 * width : 4 * width],
        wide[:, :, :experts_total],
        jnp.swapaxes(wide[:, :, experts_total : experts_total + 2], 1, 2),
        jnp.swapaxes(wide[:, :, experts_total + 2 :], 1, 2),
        grad_first,
        grad_second,
    )


def solution(mesh):

    return jax.shard_map(
        whole_step,
        mesh=mesh,
        in_specs=(
            P(("dp", "expert"), None, None),
            P(("dp", "expert"), None, None),
            P(None, "dp", None),
            P(None, "dp", None),
            P(None, "dp", None),
            P(None, None, "dp"),
            P(None, None, "dp"),
            P(None, "expert", None, "dp"),
            P(None, "expert", "dp", None),
            P(None, ("dp", "expert"), None, None),
        ),
        out_specs=(
            P(("dp", "expert"), None, None),
            P(("dp", "expert"), None, None),
            P(None, "dp", None),
            P(None, "dp", None),
            P(None, "dp", None),
            P(None, None, "dp"),
            P(None, None, "dp"),
            P(None, "expert", None, "dp"),
            P(None, "expert", "dp", None),
        ),
        check_vma=False,
    )
```

```python
import jax
import jax.numpy as jnp
from jax import lax
from jax.experimental import pallas as pl
from jax.sharding import PartitionSpec as P

HEADS = 8
HEAD_DIM = 64
SEQ = 197
SEQ_PAD = 208
LAYERS = 2
ROW_DOTS = (((1,), (1,)), ((), ()))
COL_DOTS = (((0,), (0,)), ((), ()))


EPSILON = 1e-06
ROOT_HALF = 0.7071067811865476
INV_ROOT_TAU = 0.3989422804014327


def layer_norm(values, scale_in, shift_in):
    center = values - jnp.mean(values, axis=-1, keepdims=True)
    variance = jnp.mean(center * center, axis=-1, keepdims=True)
    inverse = lax.rsqrt(variance + EPSILON)
    normed = center * inverse
    return (normed * scale_in + shift_in, normed, inverse)


def norm_back(grad_out, normed, inverse, scale_in):
    grad_normed = grad_out * scale_in
    first_mean = jnp.mean(grad_normed, axis=-1, keepdims=True)
    second_mean = jnp.mean(grad_normed * normed, axis=-1, keepdims=True)
    grad_in = inverse * (grad_normed - first_mean - normed * second_mean)
    return (grad_in, jnp.sum(grad_out * normed, axis=0), jnp.sum(grad_out, axis=0))


def softmax_rows(scores):
    highest = jnp.max(scores, axis=-1, keepdims=True)
    powers = jnp.exp(scores - highest)
    row_total = jnp.sum(powers, axis=-1, keepdims=True)
    return (powers / row_total, highest + jnp.log(row_total))


def gelu_value(preact):
    return 0.5 * preact * (1.0 + lax.erf(preact * ROOT_HALF))


def gelu_slope(preact):
    return (
        0.5 * (1.0 + lax.erf(preact * ROOT_HALF))
        + preact * jnp.exp(-0.5 * preact * preact) * INV_ROOT_TAU
    )


def gather_quarter(which, ahead, w_qkv, w_proj, w_router, norm_gains, norm_shifts):
    peers, rank = lax.axis_size("expert"), lax.axis_index("expert")
    piece = w_qkv.shape[1] // peers
    packed = jnp.concatenate(
        [
            w_qkv[which],
            w_proj[which],
            w_router[which],
            norm_gains[which].T,
            norm_shifts[which].T,
        ],
        axis=1,
    )
    block = lax.dynamic_slice_in_dim(packed, rank * piece, piece, axis=0)[None]
    block, ahead = lax.optimization_barrier((block, ahead))
    place, size, step = lax.axis_index("dp"), lax.axis_size("dp"), 2
    while step < size:
        moved = lax.ppermute(block, "dp", [(source, source ^ step) for source in range(size)])
        upper = (place // step) % 2 == 1
        first, second = jnp.where(upper, moved, block), jnp.where(upper, block, moved)
        block = jnp.concatenate([first, second], axis=0)
        step = 2 * step
    return (block, ahead)


def spread_quarter(quarter):
    parts = jnp.broadcast_to(quarter[None], (lax.axis_size("expert"),) + quarter.shape)
    return exchange(parts)


def join_cores(parts, experts):
    size = lax.axis_size("dp")
    peers, chips, rows, columns = parts.shape
    other = lax.ppermute(parts, "dp", [(source, source ^ 1) for source in range(size)])
    core = lax.axis_index("dp") % 2
    width = 2 * peers * chips * rows
    own = lax.broadcasted_iota(jnp.int32, (1, 2, 1, 1, 1), 1) == core

    def whole(start, stop):
        mine = parts[..., start:stop].swapaxes(0, 1)[:, None]
        theirs = other[..., start:stop].swapaxes(0, 1)[:, None]
        return jnp.where(own, mine, theirs).reshape(width, stop - start)

    base = 4 * width
    wide = whole(base, columns)
    gains = wide[:, experts : experts + 2].T.astype(jnp.float32)
    shifts = wide[:, experts + 2 : experts + 4].T.astype(jnp.float32)
    return (whole(0, 3 * width), whole(3 * width, base), wide[:, :experts], gains, shifts)


def owner_gates(incoming, router_full):
    logits = jnp.einsum("sjcd,de->sjce", incoming, router_full, preferred_element_type=jnp.float32)
    router_probs, _ = softmax_rows(logits)
    local = incoming.shape[1]
    own = lax.axis_index("expert") * local + jnp.arange(local, dtype=jnp.int32)
    labels = jnp.arange(router_full.shape[1], dtype=jnp.int32)
    pick = (own[:, None] == labels[None, :]).astype(jnp.float32)
    return jnp.sum(router_probs * pick[None, :, None, :], axis=-1, keepdims=True)


def gather_experts(which, w_first, w_second):
    if which == 0:
        both = jnp.stack([jnp.swapaxes(w_first[which], 1, 2), w_second[which]])
        both = lax.all_gather(both, "dp", axis=2, tiled=True)
        return (both[0], both[1])
    first_full = lax.all_gather(w_first[which], "dp", axis=2, tiled=True)
    second_full = lax.all_gather(w_second[which], "dp", axis=1, tiled=True)
    return (jnp.swapaxes(first_full, 1, 2), second_full)


def route_tables(route, experts_total, capacity):
    labels = jnp.arange(experts_total, dtype=jnp.int32)
    pick_first = (route[:, 0:1] == labels[None, :]).astype(jnp.int32)
    pick_second = (route[:, 1:2] == labels[None, :]).astype(jnp.int32)
    both_picks = pick_first + pick_second
    before = jnp.cumsum(both_picks, axis=0) - both_picks
    slot_first = route[:, 0] * capacity + jnp.sum(before * pick_first, axis=1)
    slot_second = route[:, 1] * capacity + jnp.sum(before * pick_second, axis=1)
    slot_ids = jnp.arange(experts_total * capacity, dtype=jnp.int32)
    place_first = (slot_ids[:, None] == slot_first[None, :]).astype(jnp.bfloat16)
    place_second = (slot_ids[:, None] == slot_second[None, :]).astype(jnp.bfloat16)
    return (
        pick_first.astype(jnp.float32),
        pick_second.astype(jnp.float32),
        place_first,
        place_second,
    )


def exchange(block):
    return lax.all_to_all(block, "expert", split_axis=0, concat_axis=0, tiled=True)


def head_of(ref, part, head):
    start = part * HEADS * HEAD_DIM + head * HEAD_DIM
    return ref[:, start : start + HEAD_DIM]


def masked_scores(query, keyed):
    scores = lax.dot_general(query, keyed, ROW_DOTS, preferred_element_type=jnp.float32)
    columns = lax.broadcasted_iota(jnp.int32, scores.shape, 1)
    return jnp.where(columns < SEQ, scores, -1e30)


def attention_kernel(packed_ref, mixed_ref, total_ref):
    scale = jnp.asarray(HEAD_DIM ** (-0.5), jnp.bfloat16)
    mixed, totals = [], []
    for head in range(HEADS):
        query = head_of(packed_ref, 0, head) * scale
        scores = masked_scores(query, head_of(packed_ref, 1, head))
        highest = jnp.max(scores, axis=-1, keepdims=True)
        powers = jnp.exp(scores - highest)
        row_total = jnp.sum(powers, axis=-1, keepdims=True)
        probs = (powers * (1.0 / row_total)).astype(jnp.bfloat16)
        mixed.append(
            jnp.dot(
                probs, head_of(packed_ref, 2, head), preferred_element_type=jnp.float32
            ).astype(jnp.bfloat16)
        )
        totals.append(highest + jnp.log(row_total))
    mixed_ref[...] = jnp.concatenate(mixed, axis=1)
    total_ref[...] = jnp.concatenate(totals, axis=1)


def attention_back_kernel(packed_ref, grad_ref, total_ref, out_ref):
    scale = jnp.asarray(HEAD_DIM ** (-0.5), jnp.bfloat16)
    queries, keys, values = [], [], []
    for head in range(HEADS):
        query = head_of(packed_ref, 0, head) * scale
        keyed = head_of(packed_ref, 1, head)
        grad_mixed = head_of(grad_ref, 0, head)
        scores = masked_scores(query, keyed)
        probs = jnp.exp(scores - total_ref[:, head : head + 1])
        grad_probs = lax.dot_general(
            grad_mixed,
            head_of(packed_ref, 2, head),
            ROW_DOTS,
            preferred_element_type=jnp.float32,
        )
        values.append(
            lax.dot_general(
                probs.astype(jnp.bfloat16),
                grad_mixed,
                COL_DOTS,
                preferred_element_type=jnp.float32,
            ).astype(jnp.bfloat16)
        )
        row_inner = jnp.sum(probs * grad_probs, axis=-1, keepdims=True)
        grad_scores = (probs * (grad_probs - row_inner)).astype(jnp.bfloat16)
        grad_query = jnp.dot(grad_scores, keyed, preferred_element_type=jnp.float32)
        queries.append(grad_query.astype(jnp.bfloat16) * scale)
        keys.append(
            lax.dot_general(
                grad_scores, query, COL_DOTS, preferred_element_type=jnp.float32
            ).astype(jnp.bfloat16)
        )
    out_ref[...] = jnp.concatenate(queries + keys + values, axis=1)


def image_block(columns):
    return pl.BlockSpec((SEQ_PAD, columns), lambda image: (image, 0))


def attention(packed):
    rows, columns = packed.shape
    width = columns // 3
    return pl.pallas_call(
        attention_kernel,
        grid=(rows // SEQ_PAD,),
        in_specs=[image_block(columns)],
        out_specs=[image_block(width), image_block(HEADS)],
        out_shape=[
            jax.ShapeDtypeStruct((rows, width), jnp.bfloat16),
            jax.ShapeDtypeStruct((rows, HEADS), jnp.float32),
        ],
        name="attention",
    )(packed)


def attention_back(packed, grad_mixed, totals):
    rows, columns = packed.shape
    return pl.pallas_call(
        attention_back_kernel,
        grid=(rows // SEQ_PAD,),
        in_specs=[image_block(columns), image_block(columns // 3), image_block(HEADS)],
        out_specs=image_block(columns),
        out_shape=jax.ShapeDtypeStruct((rows, columns), jnp.bfloat16),
        name="attention_back",
    )(packed, grad_mixed, totals)


def attend_forward(resid, dense, tables):
    qkv_full, proj_full, router_full, gains_wide, shifts_wide = dense
    pick_first_f, pick_second_f, _, _ = tables
    attn_norm, unit_a, inv_a = layer_norm(resid, gains_wide[0], shifts_wide[0])
    attn_in = attn_norm.astype(jnp.bfloat16)
    packed = jnp.dot(attn_in, qkv_full, preferred_element_type=jnp.float32)
    packed = packed.astype(jnp.bfloat16)
    mixed, totals = attention(packed)
    resid_mid = resid + jnp.dot(mixed, proj_full, preferred_element_type=jnp.float32)
    moe_norm, unit_b, inv_b = layer_norm(resid_mid, gains_wide[1], shifts_wide[1])
    moe_in = moe_norm.astype(jnp.bfloat16)
    logits = jnp.dot(moe_in, router_full, preferred_element_type=jnp.float32)
    router_probs, _ = softmax_rows(logits)
    gate_first = jnp.sum(router_probs * pick_first_f, axis=1)
    gate_second = jnp.sum(router_probs * pick_second_f, axis=1)
    router_probs, gate_first, gate_second = lax.optimization_barrier(
        (router_probs, gate_first, gate_second)
    )
    attn_saved = (unit_a, inv_a, attn_in, packed, totals, mixed)
    moe_saved = (unit_b, inv_b, moe_in, router_probs, gate_first, gate_second)
    return (resid_mid, attn_saved, moe_saved)


def slots_of(rows, place, block_shape):
    slots = jnp.dot(place, rows, preferred_element_type=jnp.float32)
    return slots.astype(jnp.bfloat16).reshape(block_shape)


def gated_slots(grad_out, moe_saved, tables, block_shape):
    gate_first, gate_second = moe_saved[4:]
    place_first, place_second = tables[2:]
    send_first = (gate_first[:, None] * grad_out).astype(jnp.bfloat16)
    send_second = (gate_second[:, None] * grad_out).astype(jnp.bfloat16)
    slots = jnp.dot(place_first, send_first, preferred_element_type=jnp.float32) + jnp.dot(
        place_second, send_second, preferred_element_type=jnp.float32
    )
    return slots.astype(jnp.bfloat16).reshape(block_shape)


def experts_hidden(incoming, first_full):
    hidden_pre = jnp.einsum(
        "sjcd,jfd->sjcf", incoming, first_full, preferred_element_type=jnp.float32
    )
    return (hidden_pre, gelu_value(hidden_pre).astype(jnp.bfloat16))


def experts_result(hidden_act, second_full):
    return jnp.einsum(
        "sjcf,jfd->sjcd", hidden_act, second_full, preferred_element_type=jnp.float32
    ).astype(jnp.bfloat16)


def rows_back(returned, place):
    return jnp.einsum("st,sd->td", place, returned, preferred_element_type=jnp.float32)


def experts_backward(grad_result, incoming, hidden_pre, hidden_act, experts):
    first_full, second_full = experts
    grad_second = jnp.einsum(
        "sjcf,sjcd->jfd", hidden_act, grad_result, preferred_element_type=jnp.float32
    ).astype(jnp.bfloat16)
    share_second = lax.psum_scatter(grad_second, "dp", scatter_dimension=1, tiled=True)
    grad_act = jnp.einsum(
        "sjcd,jfd->sjcf", grad_result, second_full, preferred_element_type=jnp.float32
    )
    grad_pre = (grad_act * gelu_slope(hidden_pre)).astype(jnp.bfloat16)
    grad_rows = jnp.einsum(
        "sjcf,jfd->sjcd", grad_pre, first_full, preferred_element_type=jnp.float32
    ).astype(jnp.bfloat16)
    grad_back = exchange(grad_rows)
    grad_first = jnp.einsum(
        "sjcd,sjcf->jdf", incoming, grad_pre, preferred_element_type=jnp.float32
    ).astype(jnp.bfloat16)
    grad_back, grad_first = lax.optimization_barrier((grad_back, grad_first))
    share_first = lax.psum_scatter(grad_first, "dp", scatter_dimension=2, tiled=True)
    return (grad_back, share_first, share_second)


def tokens_backward(grad_out, grad_back, backs, dense, tables, attn_saved, moe_saved):
    qkv_full, proj_full, router_full, gains_wide, _ = dense
    pick_first_f, pick_second_f, place_first, place_second = tables
    unit_a, inv_a, attn_in, packed, totals, mixed = attn_saved
    unit_b, inv_b, moe_in, router_probs, _, _ = moe_saved
    width = grad_out.shape[1]
    grad_gate_first = jnp.sum(grad_out * backs[0], axis=1)
    grad_gate_second = jnp.sum(grad_out * backs[1], axis=1)
    grad_back = grad_back.reshape(-1, width)
    grad_moe = rows_back(grad_back, place_first + place_second)
    grad_probs = pick_first_f * grad_gate_first[:, None] + pick_second_f * grad_gate_second[:, None]
    weighted = jnp.sum(router_probs * grad_probs, axis=1, keepdims=True)
    grad_logits = (router_probs * (grad_probs - weighted)).astype(jnp.bfloat16)
    grad_router = jnp.einsum("td,te->de", moe_in, grad_logits, preferred_element_type=jnp.float32)
    grad_moe = grad_moe + jnp.einsum(
        "te,de->td", grad_logits, router_full, preferred_element_type=jnp.float32
    )
    grad_norm_b, gain_b_grad, shift_b_grad = norm_back(grad_moe, unit_b, inv_b, gains_wide[1])
    grad_mid = grad_out + grad_norm_b
    grad_branch = grad_mid.astype(jnp.bfloat16)
    grad_proj = jnp.einsum("td,te->de", mixed, grad_branch, preferred_element_type=jnp.float32)
    grad_mixed = jnp.einsum("te,de->td", grad_branch, proj_full, preferred_element_type=jnp.float32)
    grad_packed = attention_back(packed, grad_mixed.astype(jnp.bfloat16), totals)
    grad_qkv = jnp.einsum("td,te->de", attn_in, grad_packed, preferred_element_type=jnp.float32)
    grad_attn = jnp.einsum("te,de->td", grad_packed, qkv_full, preferred_element_type=jnp.float32)
    grad_norm_a, gain_a_grad, shift_a_grad = norm_back(grad_attn, unit_a, inv_a, gains_wide[0])
    grad_in = grad_mid + grad_norm_a
    low = jnp.bfloat16
    small = jnp.concatenate(
        [
            grad_qkv.astype(low),
            grad_proj.astype(low),
            grad_router.astype(low),
            jnp.stack([gain_a_grad, gain_b_grad, shift_a_grad, shift_b_grad], axis=1).astype(low),
        ],
        axis=1,
    )
    peers, chips = lax.axis_size("expert"), lax.axis_size("dp") // 2
    small = small.reshape(chips, 2, peers, width // (2 * chips * peers), small.shape[1])
    small = small.transpose(1, 2, 0, 3, 4)
    return (grad_in, small)


def halve(block, bit, step):
    size = lax.axis_size("dp")
    kept = lax.dynamic_index_in_dim(block, bit, 0, keepdims=False)
    sent = lax.dynamic_index_in_dim(block, 1 - bit, 0, keepdims=False)
    moved = lax.ppermute(sent, "dp", [(source, source ^ step) for source in range(size)])
    return (kept.astype(jnp.float32) + moved.astype(jnp.float32)).astype(jnp.bfloat16)


def sum_small(small, beside):
    place = lax.axis_index("dp")
    small = halve(small, place % 2, 1)
    small = exchange(small)
    small, beside = lax.optimization_barrier((small, beside))
    small = jnp.sum(small.astype(jnp.float32), axis=0).astype(jnp.bfloat16)
    step = 2
    while small.shape[0] > 1:
        chips, rows, columns = small.shape
        block = small.reshape(chips // 2, 2, rows, columns).swapaxes(0, 1)
        small = halve(block, (place // step) % 2, step)
        step = 2 * step
    return (small[0], beside)


def whole_step(
    embedded, cotangent, w_qkv, w_proj, w_router, norm_gains, norm_shifts, w_first, w_second, routes
):
    images, length, width = embedded.shape
    tok_count = images * length
    experts_total = w_router.shape[2]
    peers = lax.axis_size("expert")
    capacity = -(-max(2, 3 * tok_count // experts_total) // 8) * 8
    block_shape = (peers, experts_total // peers, capacity, width)
    fill = ((0, 0), (0, SEQ_PAD - length), (0, 0))
    rows = images * SEQ_PAD
    cot_low = jnp.pad(cotangent, fill).reshape(rows, width)
    resid = jnp.pad(embedded, fill).reshape(rows, width).astype(jnp.float32)
    grad = cot_low.astype(jnp.float32)
    dense, experts, tables = [], [], []
    quarters = [()]
    for which in range(LAYERS):
        block, quarters[-1] = gather_quarter(
            which, quarters[-1], w_qkv, w_proj, w_router, norm_gains, norm_shifts
        )
        quarters.append(block)
    quarters = quarters[1:]
    for which in range(LAYERS):
        experts.append(gather_experts(which, w_first, w_second))
        route = jnp.pad(routes[which], fill, constant_values=experts_total).reshape(rows, 2)
        tables.append(route_tables(route, experts_total, capacity))
    last = tables[LAYERS - 1]
    slots = slots_of(cot_low, last[2] + last[3], block_shape)
    cot_rows = exchange(slots)
    parts = []
    for which in range(LAYERS):
        parts.append(spread_quarter(quarters[which]))
    dense.append(join_cores(parts[0], experts_total))
    attn_saved, moe_saved, kept = [], [], []
    grad_result = None
    for which in range(LAYERS):
        table = tables[which]
        resid_mid, attn_part, moe_part = attend_forward(resid, dense[which], table)
        if which < LAYERS - 1:
            parts[which + 1], resid_mid = lax.optimization_barrier((parts[which + 1], resid_mid))
            dense.append(join_cores(parts[which + 1], experts_total))
        outgoing = slots_of(moe_part[2], table[2] + table[3], block_shape)
        incoming = exchange(outgoing)
        hidden_pre, hidden_act = experts_hidden(incoming, experts[which][0])
        if which == LAYERS - 1:
            gates = owner_gates(incoming, dense[which][2])
            grad_result = (gates * cot_rows.astype(jnp.float32)).astype(jnp.bfloat16)
        result = experts_result(hidden_act, experts[which][1])
        returned = exchange(result).reshape(experts_total * capacity, width)
        backs = (rows_back(returned, table[2]), rows_back(returned, table[3]))
        resid = resid_mid + (
            moe_part[4][:, None] * backs[0] + moe_part[5][:, None] * backs[1]
        )
        attn_saved.append(attn_part)
        moe_saved.append(moe_part)
        kept.append((incoming, hidden_pre, hidden_act, backs))
    out_images = resid.reshape(images, SEQ_PAD, width)[:, :length].astype(jnp.bfloat16)
    smalls, firsts, seconds = [None] * LAYERS, [None] * LAYERS, [None] * LAYERS
    for which in reversed(range(LAYERS)):
        incoming, hidden_pre, hidden_act, backs = kept[which]
        if which < LAYERS - 1:
            slots = gated_slots(grad, moe_saved[which], tables[which], block_shape)
            grad_result = exchange(slots)
            grad_result, smalls[which + 1] = lax.optimization_barrier(
                (grad_result, smalls[which + 1])
            )
        grad_back, firsts[which], seconds[which] = experts_backward(
            grad_result, incoming, hidden_pre, hidden_act, experts[which]
        )
        grad, smalls[which] = tokens_backward(
            grad,
            grad_back,
            backs,
            dense[which],
            tables[which],
            attn_saved[which],
            moe_saved[which],
        )
    for which in reversed(range(LAYERS)):
        beside = jnp.stack(seconds).astype(jnp.float32) if which == 0 else ()
        smalls[which], beside = sum_small(smalls[which], beside)
    both = jnp.stack(smalls, axis=1)
    grad_first = jnp.stack(firsts).astype(jnp.float32)
    both, grad_first = lax.optimization_barrier((both, grad_first))
    total = lax.all_gather(both, "expert", axis=0, tiled=True)
    total = total.swapaxes(0, 1).astype(jnp.float32)
    grad_images = grad.reshape(images, SEQ_PAD, width)[:, :length]
    wide = total[:, :, 4 * width :]
    return (
        out_images,
        grad_images,
        total[:, :, : 3 * width],
        total[:, :, 3 * width : 4 * width],
        wide[:, :, :experts_total],
        jnp.swapaxes(wide[:, :, experts_total : experts_total + 2], 1, 2),
        jnp.swapaxes(wide[:, :, experts_total + 2 :], 1, 2),
        grad_first,
        beside,
    )


def solution(mesh):

    return jax.shard_map(
        whole_step,
        mesh=mesh,
        in_specs=(
            P(("dp", "expert"), None, None),
            P(("dp", "expert"), None, None),
            P(None, "dp", None),
            P(None, "dp", None),
            P(None, "dp", None),
            P(None, None, "dp"),
            P(None, None, "dp"),
            P(None, "expert", None, "dp"),
            P(None, "expert", "dp", None),
            P(None, ("dp", "expert"), None, None),
        ),
        out_specs=(
            P(("dp", "expert"), None, None),
            P(("dp", "expert"), None, None),
            P(None, "dp", None),
            P(None, "dp", None),
            P(None, "dp", None),
            P(None, None, "dp"),
            P(None, None, "dp"),
            P(None, "expert", None, "dp"),
            P(None, "expert", "dp", None),
        ),
        check_vma=False,
    )
```
